1024 devices in a mesh: dp: 4 (over z_hi, core), expert: 64 (over z_lo, y), tensor: 4 (over x).
Axes of the slice: x: 4, y: 8, z: 16 (z_hi: 2, z_lo: 8; z = z_hi * 8 + z_lo), core: 2. Of those that a mesh axis runs over, the one named last changes fastest.
Arguments:
- tokens: bfloat16 [16384, 3584], P(('dp', 'expert'), 'tensor'), may hold values from -6 to 6
- route_slots: int32 [16384, 8], P(('dp', 'expert')), may hold values from 0 to 63, as said below
- route_scores: float32 [16384, 8], P(('dp', 'expert')), may hold values from 0.05 to 1
- slot_expert: int32 [64], replicated, may hold values from 0 to 47, as said below
- w_in: bfloat16 [64, 3584, 2, 1024], P('expert', None, None, 'tensor'), may hold values from -6 to 6, as said below
- w_out: bfloat16 [64, 1024, 3584], P('expert', 'tensor'), may hold values from -6 to 6, as said below
Outputs:
- moe_out: bfloat16 [16384, 3584], P(('dp', 'expert'), 'tensor')
- expert_load: float32 [4, 48], P('dp')
The draws below stay inside these ranges and needn't reach their ends.
Inputs may be any that keep to these rules, and one draw needn't show every extreme that they name: `route_slots`: each row names 8 different slots. In each device's block of 64 rows no slot is named by more than 9 rows, and one slot is named by exactly 9 rows in every block. `slot_expert`: every expert is held by one or two slots; 16 experts are held by two. `w_in`: slots that hold the same expert hold equal weights. `w_out`: slots that hold the same expert hold equal weights.
All inputs are finite; a program needn't handle non-finite values.
Results may differ from the reference program's by a relative error of at most 0.012.
Values may be sent and summed in bfloat16 or wider, within the bound.
A program may use at most 64 MiB of HBM per device.

```python
import math
import jax
import jax.numpy as jnp
from jax import lax

D = 3584
F = 1024
TOP = 8
TOK_DEV = 64
SLOTS = 64
SPARE = 16
EXPERTS = 48
CAP = 9
TOKENS = 16384
N_DP = 4
N_EXPERT = 64
N_TENSOR = 4


def placement_table(key):
    base = jax.random.fold_in(key, 7)
    order = jax.random.permutation(jax.random.fold_in(base, 1), SLOTS)
    copied = jax.random.permutation(jax.random.fold_in(base, 2), EXPERTS)[:SPARE]
    held = jnp.concatenate([jnp.arange(EXPERTS, dtype=jnp.int32), copied.astype(jnp.int32)])
    return jnp.zeros((SLOTS,), jnp.int32).at[order].set(held)


def draw_slot_expert(key, part):
    return placement_table(key)


def draw_w_in(key, part):
    holder = placement_table(key)
    base = jax.random.fold_in(key, 101)

    def one_slot(expert_id):
        values = jax.random.normal(jax.random.fold_in(base, expert_id), (D, 2, F), jnp.float32)
        return (jnp.clip(values, -6.0, 6.0) * D ** (-0.5)).astype(jnp.bfloat16)
    return lax.map(one_slot, holder)


def draw_w_out(key, part):
    holder = placement_table(key)
    base = jax.random.fold_in(key, 202)

    def one_slot(expert_id):
        values = jax.random.normal(jax.random.fold_in(base, expert_id), (F, D), jnp.float32)
        return (jnp.clip(values, -6.0, 6.0) * F ** (-0.5)).astype(jnp.bfloat16)
    return lax.map(one_slot, holder)


def draw_route_slots(key, part):
    rank_key = jax.random.fold_in(key, 31)
    hot_key = jax.random.fold_in(key, 32)
    block_key = jax.random.fold_in(key, 33)
    ranking = jax.random.permutation(rank_key, SLOTS).astype(jnp.int32)
    hottest = jax.random.randint(hot_key, (), 0, SLOTS)
    pool_slot = jnp.repeat(jnp.arange(SLOTS, dtype=jnp.int32), CAP)
    pool_index = jnp.arange(SLOTS * CAP, dtype=jnp.int32)

    def one_block(block_seed):
        noise_key, row_key = jax.random.split(block_seed)
        noise = jax.random.randint(noise_key, (SLOTS * CAP,), 0, 32 * SLOTS)
        scores = noise + 16 * ranking[pool_slot]
        scores = jnp.where(pool_slot == hottest, -1, scores)
        order = jnp.argsort(scores * (SLOTS * CAP) + pool_index, stable=True)
        chosen = jnp.sort(pool_slot[order[:TOK_DEV * TOP]])
        layout = chosen.reshape(TOP, TOK_DEV).T
        shuffle = jax.random.permutation(row_key, TOK_DEV)
        return layout[shuffle]
    seeds = jax.random.split(block_key, TOKENS // TOK_DEV)
    return jax.vmap(one_block)(seeds).reshape(TOKENS, TOP).astype(jnp.int32)


def steps_of(rng, extent, cuts, least, top_value):
    def one(dim, parts):
        draws = jax.random.uniform(jax.random.fold_in(jax.random.fold_in(rng, 6), dim), (parts,), jnp.float32, least / len(cuts), top_value / len(cuts))
        return jnp.repeat(jnp.exp(draws), extent[dim] // parts).reshape((-1,) + (1,) * (len(extent) - dim - 1))

    gain = one(*cuts[0])
    for cut in cuts[1:]:
        gain = gain * one(*cut)
    return gain


def bell_draw(own_key, dims, deviation, reach, shards=(), kind=jnp.bfloat16):
    values = deviation * jax.random.normal(own_key, dims, jnp.float32)
    if shards:
        values = values * steps_of(own_key, dims, shards, -0.22, 0.18)
    return jnp.clip(values, -reach, reach).astype(kind)


def setup_inputs(seed: int = 0) -> dict:
    splits = jax.random.split(jax.random.key(seed), 7)
    return {
        "tokens": bell_draw(splits[0], (TOKENS, D), 1.0, 6.0, ((0, 256), (1, 4))),
        "route_slots": draw_route_slots(jax.random.fold_in(splits[6], 71), 0),
        "route_scores": jnp.clip(jnp.exp(math.log(1.0) - 2.9957323 * jax.random.uniform(splits[2], (TOKENS, TOP), jnp.float32) ** steps_of(splits[2], (TOKENS, TOP), ((0, 256),), -0.2, 0.2)), 0.05, 1.0),
        "slot_expert": draw_slot_expert(jax.random.fold_in(splits[6], 71), 0),
        "w_in": draw_w_in(jax.random.fold_in(splits[6], 71), 0),
        "w_out": draw_w_out(jax.random.fold_in(splits[6], 71), 0),
    }


ROUTED = 2.5


def reference(tokens, route_slots, route_scores, slot_expert, w_in, w_out):
    gates = route_scores / jnp.sum(route_scores, axis=1, keepdims=True) * ROUTED
    flat_slot = route_slots.reshape(-1)
    flat_gate = gates.reshape(-1)
    token_of = (jnp.arange(TOKENS * TOP, dtype=jnp.int32) // TOP).astype(jnp.int32)
    most_rows = N_DP * N_EXPERT * CAP
    part_units = F // N_TENSOR

    def one_slot(running, slot_id):
        chosen = flat_slot == slot_id
        position = jnp.cumsum(chosen.astype(jnp.int32)) - 1
        landing = jnp.where(chosen, position, most_rows).astype(jnp.int32)
        picked = jnp.zeros((most_rows,), jnp.int32).at[landing].set(token_of, mode="drop")
        weight = jnp.zeros((most_rows,), jnp.float32).at[landing].set(flat_gate, mode="drop")
        gathered = tokens[picked]
        w_first = w_in[slot_id].reshape(D, 2 * F)
        projected = jnp.dot(gathered, w_first, preferred_element_type=jnp.float32).reshape(most_rows, 2, F)
        hidden = (jax.nn.silu(projected[:, 0]) * projected[:, 1]).astype(jnp.bfloat16)
        w_second = w_out[slot_id]
        summed = jnp.zeros((most_rows, D), jnp.float32)
        for tensor_part in range(N_TENSOR):
            first_unit = tensor_part * part_units
            partial_value = jnp.dot(hidden[:, first_unit:first_unit + part_units], w_second[first_unit:first_unit + part_units], preferred_element_type=jnp.float32)
            rounded = lax.optimization_barrier(partial_value.astype(jnp.bfloat16))
            summed = summed + rounded.astype(jnp.float32)
        expert_out = lax.optimization_barrier(summed.astype(jnp.bfloat16))
        running = running.at[picked].add(weight[:, None] * expert_out.astype(jnp.float32))
        return running, None

    running, unused = lax.scan(one_slot, jnp.zeros((TOKENS, D), jnp.float32), jnp.arange(SLOTS, dtype=jnp.int32))
    moe_out = running.astype(jnp.bfloat16)
    matches = route_slots.reshape(N_DP, -1)[:, :, None] == jnp.arange(SLOTS, dtype=jnp.int32)[None, None, :]
    slot_totals = jnp.sum(jnp.where(matches, gates.reshape(N_DP, -1)[:, :, None], 0.0), axis=1)
    holder = (slot_expert[:, None] == jnp.arange(EXPERTS, dtype=jnp.int32)[None, :]).astype(jnp.float32)
    expert_load = jnp.sum(slot_totals[:, :, None] * holder[None], axis=1) * (EXPERTS / (N_EXPERT * TOK_DEV * ROUTED))
    return moe_out, expert_load
```

```python
import functools

import jax
import jax.numpy as jnp
from jax import lax
from jax.experimental import pallas as pl
from jax.experimental.pallas import tpu as pltpu
from jax.sharding import PartitionSpec as P

ROUTED = 2.5
MESH = pl.DeviceIdType.MESH


class Plan:
    def __init__(self, nz, ny, tok, top, width, hidden, experts, scale, cuts):
        self.nz, self.ny, self.tok, self.top = nz, ny, tok, top
        self.slots = nz * ny
        self.cap = 9 * tok * top // (8 * self.slots)
        self.rows = nz * self.cap
        self.all_rows = ny * self.rows
        self.width, self.hidden = width, hidden
        self.experts, self.scale = experts, scale
        self.cuts = cuts


def layer_kernel(
    p,
    tok_ref, meta_ref, held_ref, win_ref, wout_ref,
    out_ref, load_ref,
    tokens, metas, sel, selg, outgo, gath, proj, hid, wcols, relay, wfirst,
    result, back, part, carry, passed, loads,
    z_send, z_recv, m_send, m_recv, y_send, y_recv, x_send, x_recv,
    h_send, h_recv, w_send, w_recv, b_send, b_recv, c_send, c_recv, l_send, l_recv, own,
):
    NZ, NY, T = p.nz, p.ny, p.tok
    W, F = p.width, p.hidden
    e = lax.axis_index("expert")
    x = lax.axis_index("tensor")
    z = e // NY
    y = e % NY
    right, left, across = (x + 1) % 4, (x + 3) % 4, (x + 2) % 4
    cuts = p.cuts
    last = len(cuts)
    HY = NY // 2

    def remote(src, dst, send, recv, dev):
        return pltpu.make_async_remote_copy(
            src_ref=src, dst_ref=dst, send_sem=send, recv_sem=recv, device_id=dev, device_id_type=MESH
        )

    def at_z(k):
        return {"expert": k * NY + y}

    def at_y(k):
        return {"expert": z * NY + k}

    sent = []

    barrier = pltpu.get_barrier_semaphore()

    @pl.when(z > 0)
    def _():
        pl.semaphore_signal(barrier, inc=1, device_id=at_z(z - 1), device_id_type=MESH)

    @pl.when(z < NZ - 1)
    def _():
        pl.semaphore_signal(barrier, inc=1, device_id=at_z(z + 1), device_id_type=MESH)

    for j in range(1, NY):
        pl.semaphore_signal(barrier, inc=1, device_id=at_y((y + j) % NY), device_id_type=MESH)
    for n in (right, left):
        pl.semaphore_signal(barrier, inc=1, device_id={"tensor": n}, device_id_type=MESH)

    own_meta = pltpu.make_async_copy(meta_ref, metas.at[z], own.at[0])
    own_tok = pltpu.make_async_copy(tok_ref, tokens.at[z], own.at[1])
    own_wcols = pltpu.make_async_copy(wout_ref.at[:, pl.ds(pl.multiple_of(x * W, 128), W)], wcols.at[x], own.at[2])
    own_win = pltpu.make_async_copy(win_ref, wfirst, own.at[3])
    own_meta.start()
    own_tok.start()
    own_wcols.start()
    own_win.start()

    n_wait = (NY - 1) + 2 + jnp.where(z > 0, 1, 0) + jnp.where(z < NZ - 1, 1, 0)
    pl.semaphore_wait(barrier, n_wait)

    def z_step(src_of, dst_of, send, recv, d):
        up_from = z - d
        down_from = z + d
        up = remote(src_of(up_from), dst_of(up_from), send.at[0, d], recv.at[0, d + 1], at_z(z + 1))
        down = remote(src_of(down_from), dst_of(down_from), send.at[1, d], recv.at[1, d + 1], at_z(z - 1))
        return ((up, (up_from >= 0) & (z < NZ - 1)), (down, (down_from < NZ) & (z > 0)))

    def z_arrive(dst_of, recv, d):
        @pl.when(z - d >= 0)
        def _():
            remote(dst_of(z - d), dst_of(z - d), recv.at[0, d], recv.at[0, d], at_z(z)).wait_recv()

        @pl.when(z + d < NZ)
        def _():
            remote(dst_of(z + d), dst_of(z + d), recv.at[1, d], recv.at[1, d], at_z(z)).wait_recv()

    def start_if(pairs):
        for copy, cond in pairs:
            pl.when(cond)(copy.start)
            sent.append((copy, cond))

    def meta_of(k):
        return metas.at[k]

    def tok_of(f):
        c0, w = cuts[f]
        return lambda k: tokens.at[k, :, pl.ds(c0, w)]

    def tok_in(f):
        c0, w = cuts[f]
        return lambda k: tok_ref.at[:, pl.ds(c0, w)]

    start_if(z_step(lambda k: meta_ref, meta_of, m_send, m_recv, 0))

    def wblock(k, r0, n):
        return wout_ref.at[pl.ds(r0, n), pl.ds(pl.multiple_of(k * W, 128), W)]

    FH = F // 2
    w_copies = [
        remote(wblock(across, 0, FH), relay.at[0], w_send.at[0], w_recv.at[0], {"tensor": right}),
        remote(wblock(across, FH, FH), relay.at[1], w_send.at[1], w_recv.at[1], {"tensor": left}),
        remote(wblock(right, 0, F), wcols.at[x], w_send.at[2], w_recv.at[2], {"tensor": right}),
        remote(wblock(left, 0, F), wcols.at[x], w_send.at[3], w_recv.at[3], {"tensor": left}),
    ]
    w_relays = [
        remote(relay.at[0], wcols.at[left, pl.ds(0, FH)], w_send.at[4], w_recv.at[4], {"tensor": right}),
        remote(relay.at[1], wcols.at[right, pl.ds(FH, FH)], w_send.at[5], w_recv.at[5], {"tensor": left}),
    ]

    def routes():
        own_meta.wait()
        lane = lax.broadcasted_iota(jnp.int32, (p.top, 2 * T), 1)
        slots, gates = [], []
        for k in range(0, NZ, 2):
            a, b = metas[k], metas[k + 1]
            slots.append(jnp.where(lane < T, a[: p.top], b[: p.top]))
            gates.append(jnp.where(lane < T, a[p.top :], b[p.top :]))
        slots = jnp.concatenate(slots, axis=1).astype(jnp.int32)
        gates = jnp.concatenate(gates, axis=1)
        L = NZ * T
        mine = lax.broadcasted_iota(jnp.int32, (NY, L), 0) + z * NY
        match = jnp.zeros((NY, L), jnp.float32)
        gate = jnp.zeros((NY, L), jnp.float32)
        for k in range(p.top):
            eq = slots[k : k + 1] == mine
            match = match + jnp.where(eq, 1.0, 0.0)
            gate = gate + jnp.where(eq, gates[k : k + 1], 0.0)
        i0 = lax.broadcasted_iota(jnp.int32, (L, L), 0)
        i1 = lax.broadcasted_iota(jnp.int32, (L, L), 1)
        before = jnp.where((i0 < i1) & (i0 // T == i1 // T), 1.0, 0.0).astype(jnp.bfloat16)
        rank = jnp.dot(match.astype(jnp.bfloat16), before, preferred_element_type=jnp.float32)
        block = lax.broadcasted_iota(jnp.int32, (NY, L), 1) // T
        key = jnp.where(match > 0.5, rank.astype(jnp.int32) * NZ + block, -1)
        place = lax.broadcasted_iota(jnp.int32, (p.rows, L), 0)
        for k in range(NY):
            hit = key[k : k + 1] == place
            sel[k] = jnp.where(hit, 1.0, 0.0).astype(jnp.bfloat16)
            selg[k] = jnp.where(hit, gate[k : k + 1], 0.0).astype(jnp.bfloat16)
        every = lax.broadcasted_iota(jnp.int32, (p.slots, L), 0)
        total = jnp.zeros((p.slots, L), jnp.float32)
        for k in range(p.top):
            total = total + jnp.where(slots[k : k + 1] == every, gates[k : k + 1], 0.0)
        total = jnp.sum(total, axis=1, keepdims=True)
        holds = held_ref[...] == lax.broadcasted_iota(jnp.int32, (p.slots, 128), 1)
        row = jnp.sum(jnp.where(holds, total, 0.0), axis=0, keepdims=True)
        loads[y] = jnp.broadcast_to(row, (8, 128))
        for j in range(1, NY):
            copy = remote(loads.at[y], loads.at[y], l_send.at[j], l_recv.at[j], at_y((y + j) % NY))
            copy.start()
            sent.append((copy, None))

    def y_out(f):
        c0, w = cuts[f]
        block = tokens[:, :, c0 : c0 + w].reshape(NZ * T, w)
        for k in range(NY):
            outgo[k, :, c0 : c0 + w] = jnp.dot(sel[k], block, preferred_element_type=jnp.float32).astype(jnp.bfloat16)
        for j in range(1, NY):
            k = (y + j) % NY
            copy = remote(
                outgo.at[k, :, pl.ds(c0, w)], gath.at[x, y, :, pl.ds(c0, w)],
                y_send.at[f, j], y_recv.at[f, j], at_y(k),
            )
            copy.start()
            sent.append((copy, None))
        gath[x, y, :, c0 : c0 + w] = outgo[y, :, c0 : c0 + w]

    z_ready = []
    for tick in range(last + NZ - 1):
        if tick < last:
            start_if(z_step(tok_in(tick), tok_of(tick), z_send.at[tick], z_recv.at[tick], 0))
        if tick == 0:
            for copy in w_copies:
                copy.start()
                sent.append((copy, None))
        if 1 <= tick < NZ:
            z_arrive(meta_of, m_recv, tick)
            if tick < NZ - 1:
                start_if(z_step(meta_of, meta_of, m_send, m_recv, tick))
        for d in range(1, NZ):
            f = tick - d
            if 0 <= f < last:
                z_arrive(tok_of(f), z_recv.at[f], d)
                if d < NZ - 1:
                    start_if(z_step(tok_of(f), tok_of(f), z_send.at[f], z_recv.at[f], d))
        if tick == NZ - 1:
            routes()
            own_tok.wait()
        f = tick - (NZ - 1)
        if f >= 0:
            y_out(f)

    def x_out(f):
        c0, w = cuts[f]
        for j in range(1, NY):
            dst = gath.at[x, (y - j + NY) % NY, :, pl.ds(c0, w)]
            remote(dst, dst, y_recv.at[f, j], y_recv.at[f, j], at_y(y)).wait_recv()
        lo = gath.at[x, pl.ds(0, HY), :, pl.ds(c0, w)]
        hi = gath.at[x, pl.ds(HY, NY - HY), :, pl.ds(c0, w)]
        for n, (part_ref, to) in enumerate(((lo, right), (hi, left), (hi, right), (lo, left))):
            copy = remote(part_ref, part_ref, x_send.at[f, n], x_recv.at[f, n], {"tensor": to})
            copy.start()
            sent.append((copy, None))

    def x_wait(f, n, origin, low):
        c0, w = cuts[f]
        dst = gath.at[origin, pl.ds(0, HY) if low else pl.ds(HY, NY - HY), :, pl.ds(c0, w)]
        remote(dst, dst, x_recv.at[f, n], x_recv.at[f, n], {"tensor": x}).wait_recv()
        return dst

    def x_pass(f):
        got = x_wait(f, 0, left, True)
        copy = remote(got, got, x_send.at[f, 4], x_recv.at[f, 4], {"tensor": right})
        copy.start()
        sent.append((copy, None))
        got = x_wait(f, 1, right, False)
        copy = remote(got, got, x_send.at[f, 5], x_recv.at[f, 5], {"tensor": left})
        copy.start()
        sent.append((copy, None))

    def project(f):
        c0, w = cuts[f]
        x_wait(f, 2, left, False)
        x_wait(f, 3, right, True)
        x_wait(f, 4, across, True)
        x_wait(f, 5, across, False)
        total = proj[...] if f else None
        for o in range(4):
            term = jnp.dot(
                gath[o, :, :, c0 : c0 + w].reshape(p.all_rows, w),
                wfirst[o * W + c0 : o * W + c0 + w, :],
                preferred_element_type=jnp.float32,
            )
            total = term if total is None else total + term
        proj[...] = total

    for n, copy in enumerate(w_copies[:2]):
        copy.wait_recv()
        w_relays[n].start()
        sent.append((w_relays[n], None))
    own_win.wait()
    for f in range(last + 1):
        if f < last:
            x_out(f)
            x_pass(f)
        if f >= 1:
            project(f - 1)

    gate_part = proj[:, :F]
    value = gate_part / (1.0 + jnp.exp(-gate_part)) * proj[:, F:]
    hid[x] = value.astype(jnp.bfloat16)
    HR = p.all_rows // 2

    def h_half(o, low):
        return hid.at[o, pl.ds(0 if low else HR, HR)]

    def h_wait(n, o, low):
        remote(h_half(o, low), h_half(o, low), h_recv.at[n], h_recv.at[n], {"tensor": x}).wait_recv()

    def h_go(n, o, low, to):
        copy = remote(h_half(o, low), h_half(o, low), h_send.at[n], h_recv.at[n], {"tensor": to})
        copy.start()
        sent.append((copy, None))

    h_go(0, x, True, right)
    h_go(1, x, False, left)
    h_go(2, x, False, right)
    h_go(3, x, True, left)
    for copy in (w_copies[2], w_copies[3], w_relays[0], w_relays[1]):
        copy.wait_recv()
    own_wcols.wait()
    h_wait(0, left, True)
    h_go(4, left, True, right)
    h_wait(1, right, False)
    h_go(5, right, False, left)
    h_wait(2, left, False)
    h_wait(3, right, True)
    h_wait(4, across, True)
    h_wait(5, across, False)

    for f in range(last):
        c0, w = cuts[f]
        total = None
        for o in range(4):
            term = jnp.dot(hid[o], wcols[o, :, c0 : c0 + w], preferred_element_type=jnp.float32)
            total = term if total is None else total + term
        result[:, :, c0 : c0 + w] = total.astype(jnp.bfloat16).reshape(NY, p.rows, w)
        for j in range(1, NY):
            k = (y + j) % NY
            copy = remote(
                result.at[k, :, pl.ds(c0, w)], back.at[y, :, pl.ds(c0, w)],
                b_send.at[f, j], b_recv.at[f, j], at_y(k),
            )
            copy.start()
            sent.append((copy, None))
        back[y, :, c0 : c0 + w] = result[y, :, c0 : c0 + w]

    def combine(f):
        c0, w = cuts[f]
        for j in range(1, NY):
            dst = back.at[(y - j + NY) % NY, :, pl.ds(c0, w)]
            remote(dst, dst, b_recv.at[f, j], b_recv.at[f, j], at_y(y)).wait_recv()
        value = lax.dot_general(
            selg[...].reshape(p.all_rows, NZ * T),
            back[:, :, c0 : c0 + w].reshape(p.all_rows, w),
            (((0,), (0,)), ((), ())),
            preferred_element_type=jnp.float32,
        )
        part[:, :, c0 : c0 + w] = value.reshape(NZ, T, w)

    def chain(f, way):
        c0, w = cuts[f]
        step = 1 - 2 * way
        place = z + way * (NZ - 1 - 2 * z)
        for d in range(NZ - 1, 0, -1):
            to = z + step * d

            @pl.when(place + d < NZ)
            def _():
                piece = carry.at[way, to, :, pl.ds(c0, w)]

                @pl.when(place > 0)
                def _():
                    remote(piece, piece, c_recv.at[way, f, d], c_recv.at[way, f, d], at_z(z)).wait_recv()
                    passed[way, to, :, c0 : c0 + w] = (
                        carry[way, to, :, c0 : c0 + w].astype(jnp.float32) + part[to, :, c0 : c0 + w]
                    ).astype(jnp.bfloat16)

                @pl.when(place == 0)
                def _():
                    passed[way, to, :, c0 : c0 + w] = part[to, :, c0 : c0 + w].astype(jnp.bfloat16)

                chain_copy(f, way, d).start()

    def chain_copy(f, way, d):
        c0, w = cuts[f]
        step = 1 - 2 * way
        to = z + step * d
        return remote(
            passed.at[way, to, :, pl.ds(c0, w)], carry.at[way, to, :, pl.ds(c0, w)],
            c_send.at[way, f, d], c_recv.at[way, f, d - 1], at_z(z + step),
        )

    def finish(f):
        c0, w = cuts[f]
        for way in (0, 1):
            @pl.when((z > 0) if way == 0 else (z < NZ - 1))
            def _(way=way):
                piece = carry.at[way, z, :, pl.ds(c0, w)]
                remote(piece, piece, c_recv.at[way, f, 0], c_recv.at[way, f, 0], at_z(z)).wait_recv()
                part[z, :, c0 : c0 + w] = part[z, :, c0 : c0 + w] + carry[way, z, :, c0 : c0 + w].astype(jnp.float32)

        out_ref[:, c0 : c0 + w] = part[z, :, c0 : c0 + w].astype(jnp.bfloat16)

    near = jnp.where(z < NZ // 2, 0, 1)
    for f in range(last + 1):
        if f < last:
            combine(f)
            chain(f, near)
        if f >= 1:
            chain(f - 1, 1 - near)
    for f in range(last):
        finish(f)

    for j in range(1, NY):
        dst = loads.at[(y - j + NY) % NY]
        remote(dst, dst, l_recv.at[j], l_recv.at[j], at_y(y)).wait_recv()
    load_ref[...] = (jnp.sum(loads[...], axis=0) * p.scale)[0:1, : p.experts]

    for copy, cond in sent:
        if cond is None:
            copy.wait_send()
        else:
            pl.when(cond)(copy.wait_send)
    for f in range(last):
        for way in (0, 1):
            place = z + way * (NZ - 1 - 2 * z)
            for d in range(NZ - 1, 0, -1):
                pl.when(place + d < NZ)(chain_copy(f, way, d).wait_send)


def cut_columns(width):
    cuts, c0 = [], 0
    first = width % 256 or 256
    while c0 < width:
        w = first if c0 == 0 else 256
        cuts.append((c0, w))
        c0 += w
    return tuple(cuts)


def shards(nz, ny, tokens, route_slots, route_scores, slot_expert, w_in, w_out):
    tok, width = tokens.shape
    top = route_slots.shape[1]
    _, full, _, hidden = w_in.shape
    slots = nz * ny
    experts = slots - slots // 4
    p = Plan(nz, ny, tok, top, width, hidden, experts, experts / (slots * tok * ROUTED), cut_columns(width))
    gates = route_scores / jnp.sum(route_scores, axis=1, keepdims=True) * ROUTED
    meta = jnp.concatenate([route_slots.astype(jnp.float32).T, gates.T], axis=0)
    meta = jnp.concatenate([meta, meta], axis=1)
    first = w_in.reshape(full, 2 * hidden)
    n = len(p.cuts)
    bf, f32 = jnp.bfloat16, jnp.float32
    dma = pltpu.SemaphoreType.DMA
    R, A = p.rows, p.all_rows
    vmem = pl.BlockSpec(memory_space=pltpu.VMEM)
    anyspace = pl.BlockSpec(memory_space=pl.ANY)
    moe_out, load = pl.pallas_call(
        functools.partial(layer_kernel, p),
        out_shape=(
            jax.ShapeDtypeStruct((tok, width), bf),
            jax.ShapeDtypeStruct((1, experts), f32),
        ),
        in_specs=[vmem, vmem, vmem, anyspace, anyspace],
        out_specs=(vmem, vmem),
        scratch_shapes=[
            pltpu.VMEM((nz, tok, width), bf),
            pltpu.VMEM((nz, 2 * top, 2 * tok), f32),
            pltpu.VMEM((ny, R, nz * tok), bf),
            pltpu.VMEM((ny, R, nz * tok), bf),
            pltpu.VMEM((ny, R, width), bf),
            pltpu.VMEM((4, ny, R, width), bf),
            pltpu.VMEM((A, 2 * hidden), f32),
            pltpu.VMEM((4, A, hidden), bf),
            pltpu.VMEM((4, hidden, width), bf),
            pltpu.VMEM((2, hidden // 2, width), bf),
            pltpu.VMEM((full, 2 * hidden), bf),
            pltpu.VMEM((ny, R, width), bf),
            pltpu.VMEM((ny, R, width), bf),
            pltpu.VMEM((nz, tok, width), f32),
            pltpu.VMEM((2, nz, tok, width), bf),
            pltpu.VMEM((2, nz, tok, width), bf),
            pltpu.VMEM((ny, 8, 128), f32),
            dma((n, 2, nz)), dma((n, 2, nz)),
            dma((2, nz)), dma((2, nz)),
            dma((n, ny)), dma((n, ny)),
            dma((n, 6)), dma((n, 6)),
            dma((6,)), dma((6,)),
            dma((6,)), dma((6,)),
            dma((n, ny)), dma((n, ny)),
            dma((2, n, nz)), dma((2, n, nz)),
            dma((ny,)), dma((ny,)),
            dma((4,)),
        ],
        compiler_params=pltpu.CompilerParams(
            collective_id=0, has_side_effects=True, vmem_limit_bytes=60 * 1024 * 1024
        ),
    )(tokens, meta, slot_expert[:, None], first, w_out[0])
    return moe_out, load


def solution(mesh, nz=8):
    ny = mesh.shape["expert"] // nz
    placed = (
        P(("dp", "expert"), "tensor"),
        P(("dp", "expert"), None),
        P(("dp", "expert"), None),
        P(),
        P("expert", None, None, "tensor"),
        P("expert", "tensor", None),
    )
    return jax.shard_map(
        functools.partial(shards, nz, ny),
        mesh=mesh,
        in_specs=placed,
        out_specs=(P(("dp", "expert"), "tensor"), P("dp", None)),
        check_vma=False,
    )
```

```python
import functools

import jax
import jax.numpy as jnp
from jax import lax
from jax.experimental import pallas as pl
from jax.experimental.pallas import tpu as pltpu
from jax.sharding import PartitionSpec as P

ROUTED = 2.5
MESH = pl.DeviceIdType.MESH


class Plan:
    def __init__(self, nz, ny, tok, top, width, hidden, experts, scale):
        self.nz, self.ny, self.tok, self.top = nz, ny, tok, top
        self.slots = nz * ny
        self.cap = 9 * tok * top // (8 * self.slots)
        self.rows = nz * self.cap
        self.all_rows = ny * self.rows
        self.width, self.hidden = width, hidden
        self.experts, self.scale = experts, scale
        self.cut = 128
        self.cuts = width // self.cut


def layer_kernel(
    p,
    tok_ref, slots_ref, scores_ref, held_ref, win_ref, wout_ref,
    out_ref, load_ref,
    mine_meta, tokens, metas, sel, selg, selgt, outgo, gath, proj, hid, wcols, relay, wfirst,
    result, back, part, carry, passed, loads,
    z_send, z_recv, m_send, m_recv, y_send, y_recv, x_send, x_recv,
    h_send, h_recv, w_send, w_recv, b_send, b_recv, c_send, c_recv, l_send, l_recv, own,
):
    NZ, NY, T = p.nz, p.ny, p.tok
    W, F, C, N = p.width, p.hidden, p.cut, p.cuts
    L = NZ * T
    e = lax.axis_index("expert")
    x = lax.axis_index("tensor")
    z = e // NY
    y = e % NY
    right, left, across = (x + 1) % 4, (x + 3) % 4, (x + 2) % 4
    HY = NY // 2

    def remote(src, dst, send, recv, dev):
        return pltpu.make_async_remote_copy(
            src_ref=src, dst_ref=dst, send_sem=send, recv_sem=recv, device_id=dev, device_id_type=MESH
        )

    def arrive(dst, recv):
        remote(dst, dst, recv, recv, {"tensor": right}).wait_recv()

    def at_z(k):
        return {"expert": k * NY + y}

    def at_y(k):
        return {"expert": z * NY + k}

    def every(lo, hi, body):
        def step(i, c):
            body(i)
            return c

        lax.fori_loop(lo, hi, step, 0)

    barrier = pltpu.get_barrier_semaphore()

    @pl.when(z > 0)
    def _():
        pl.semaphore_signal(barrier, inc=1, device_id=at_z(z - 1), device_id_type=MESH)

    @pl.when(z < NZ - 1)
    def _():
        pl.semaphore_signal(barrier, inc=1, device_id=at_z(z + 1), device_id_type=MESH)

    for j in range(1, NY):
        pl.semaphore_signal(barrier, inc=1, device_id=at_y((y + j) % NY), device_id_type=MESH)
    for n in (right, left):
        pl.semaphore_signal(barrier, inc=1, device_id={"tensor": n}, device_id_type=MESH)

    own_wcols = pltpu.make_async_copy(wout_ref.at[:, pl.ds(pl.multiple_of(x * W, 128), W)], wcols.at[x], own.at[0])
    own_win = pltpu.make_async_copy(win_ref, wfirst, own.at[1])
    own_wcols.start()
    own_win.start()

    scores = scores_ref[...]
    gates = scores / jnp.sum(scores, axis=0, keepdims=True) * ROUTED
    names = slots_ref[...].astype(jnp.float32)
    for at in (0, T):
        mine_meta[: p.top, at : at + T] = names
        mine_meta[p.top :, at : at + T] = gates
    metas[z] = mine_meta[...]
    for f in range(N):
        tokens[f, z] = tok_ref[:, f * C : (f + 1) * C]

    n_wait = (NY - 1) + 2 + jnp.where(z > 0, 1, 0) + jnp.where(z < NZ - 1, 1, 0)
    pl.semaphore_wait(barrier, n_wait)

    def z_copies(src_of, dst_of, send, recv, d):
        return (
            (remote(src_of(z - d), dst_of(z - d), send(0, d), recv(0, d + 1), at_z(z + 1)), (z - d >= 0) & (z < NZ - 1)),
            (remote(src_of(z + d), dst_of(z + d), send(1, d), recv(1, d + 1), at_z(z - 1)), (z + d < NZ) & (z > 0)),
        )

    def z_arrive(dst_of, recv, d):
        pl.when(z - d >= 0)(lambda: arrive(dst_of(z - d), recv(0, d)))
        pl.when(z + d < NZ)(lambda: arrive(dst_of(z + d), recv(1, d)))

    def begin(pairs):
        for copy, cond in pairs:
            pl.when(cond)(copy.start)

    def left_all(pairs):
        for copy, cond in pairs:
            pl.when(cond)(copy.wait_send)

    def meta_copies(d, first=False):
        return z_copies(
            (lambda k: mine_meta) if first else (lambda k: metas.at[k]), lambda k: metas.at[k],
            lambda way, k: m_send.at[way, k], lambda way, k: m_recv.at[way, k], d,
        )

    def tok_copies(f, d, first=False):
        return z_copies(
            (lambda k: tok_ref.at[:, pl.ds(pl.multiple_of(f * C, C), C)]) if first else (lambda k: tokens.at[f, k]),
            lambda k: tokens.at[f, k],
            lambda way, k: z_send.at[f, way, k], lambda way, k: z_recv.at[f, way, k], d,
        )

    def wblock(k, r0, n):
        return wout_ref.at[pl.ds(r0, n), pl.ds(pl.multiple_of(k * W, 128), W)]

    FH = F // 2
    w_copies = [
        remote(wblock(across, 0, FH), relay.at[0], w_send.at[0], w_recv.at[0], {"tensor": right}),
        remote(wblock(across, FH, FH), relay.at[1], w_send.at[1], w_recv.at[1], {"tensor": left}),
        remote(wblock(right, 0, F), wcols.at[x], w_send.at[2], w_recv.at[2], {"tensor": right}),
        remote(wblock(left, 0, F), wcols.at[x], w_send.at[3], w_recv.at[3], {"tensor": left}),
        remote(relay.at[0], wcols.at[left, pl.ds(0, FH)], w_send.at[4], w_recv.at[4], {"tensor": right}),
        remote(relay.at[1], wcols.at[right, pl.ds(FH, FH)], w_send.at[5], w_recv.at[5], {"tensor": left}),
    ]

    def line_routes():
        lane = lax.broadcasted_iota(jnp.int32, (p.top, 2 * T), 1)
        slots, gates = [], []
        for k in range(0, NZ, 2):
            a, b = metas[k], metas[k + 1]
            slots.append(jnp.where(lane < T, a[: p.top], b[: p.top]))
            gates.append(jnp.where(lane < T, a[p.top :], b[p.top :]))
        return jnp.concatenate(slots, axis=1).astype(jnp.int32), jnp.concatenate(gates, axis=1)

    def choose():
        slots, gates = line_routes()
        mine = lax.broadcasted_iota(jnp.int32, (NY, L), 0) + z * NY
        match = jnp.zeros((NY, L), jnp.float32)
        gate = jnp.zeros((NY, L), jnp.float32)
        for k in range(p.top):
            eq = slots[k : k + 1] == mine
            match = match + jnp.where(eq, 1.0, 0.0)
            gate = gate + jnp.where(eq, gates[k : k + 1], 0.0)
        i0 = lax.broadcasted_iota(jnp.int32, (L, L), 0)
        i1 = lax.broadcasted_iota(jnp.int32, (L, L), 1)
        before = jnp.where((i0 < i1) & (i0 // T == i1 // T), 1.0, 0.0).astype(jnp.bfloat16)
        rank = jnp.dot(match.astype(jnp.bfloat16), before, preferred_element_type=jnp.float32)
        block = lax.broadcasted_iota(jnp.int32, (NY, L), 1) // T
        key = jnp.where(match > 0.5, rank.astype(jnp.int32) * NZ + block, -1)
        place = lax.broadcasted_iota(jnp.int32, (p.rows, L), 0)
        for k in range(NY):
            hit = key[k : k + 1] == place
            rows = pl.ds(k * p.rows, p.rows)
            sel[rows] = jnp.where(hit, 1.0, 0.0).astype(jnp.bfloat16)
            selg[rows] = jnp.where(hit, gate[k : k + 1], 0.0)

    def load_copy(j):
        return remote(loads.at[y], loads.at[y], l_send.at[j], l_recv.at[j], at_y((y + j) % NY))

    def weigh():
        slots, gates = line_routes()
        names = lax.broadcasted_iota(jnp.int32, (p.slots, L), 0)
        total = jnp.zeros((p.slots, L), jnp.float32)
        for k in range(p.top):
            total = total + jnp.where(slots[k : k + 1] == names, gates[k : k + 1], 0.0)
        total = jnp.broadcast_to(jnp.sum(total, axis=1, keepdims=True), (p.slots, 128))
        expert = lax.broadcasted_iota(jnp.int32, (1, 128), 1)
        row = jnp.zeros((1, 128), jnp.float32)
        for s in range(p.slots):
            row = row + jnp.where(expert == held_ref[s], total[s : s + 1], 0.0)
        loads[y] = jnp.broadcast_to(row, (8, 128))
        for j in range(1, NY):
            load_copy(j).start()
        selgt[...] = jnp.transpose(selg[...], (1, 0)).astype(jnp.bfloat16)

    def y_copy(f, j):
        k = (y + j) % NY
        return remote(outgo.at[f, k], gath.at[x, f, y], y_send.at[f, j], y_recv.at[f, j], at_y(k))

    def y_out(f):
        rows = jnp.dot(sel[...], tokens[f].reshape(L, C), preferred_element_type=jnp.float32)
        outgo[f] = rows.astype(jnp.bfloat16).reshape(NY, p.rows, C)
        for j in range(1, NY):
            y_copy(f, j).start()
        gath[x, f, y] = outgo[f, y]

    def half(o, f, low):
        return gath.at[o, f, pl.ds(0 if low else HY, HY)]

    def x_copy(f, n):
        o, low, to = (
            (x, True, right), (x, False, left), (x, False, right), (x, True, left), (left, True, right), (right, False, left)
        )[n]
        return remote(half(o, f, low), half(o, f, low), x_send.at[f, n], x_recv.at[f, n], {"tensor": to})

    def x_arrive(f, n):
        o, low = ((left, True), (right, False), (left, False), (right, True), (across, True), (across, False))[n]
        arrive(half(o, f, low), x_recv.at[f, n])

    def x_out(f):
        for j in range(1, NY):
            arrive(gath.at[x, f, (y - j + NY) % NY], y_recv.at[f, j])
        for n in range(4):
            x_copy(f, n).start()

    def x_pass(f):
        x_arrive(f, 0)
        x_copy(f, 4).start()
        x_arrive(f, 1)
        x_copy(f, 5).start()

    def project(f):
        for n in range(2, 6):
            x_arrive(f, n)
        total = proj[...]
        for o in range(4):
            total = total + jnp.dot(
                gath[o, f].reshape(p.all_rows, C),
                wfirst[pl.ds(pl.multiple_of(o * W + f * C, C), C), :],
                preferred_element_type=jnp.float32,
            )
        proj[...] = total

    begin(meta_copies(0, True))
    proj[...] = jnp.zeros_like(proj)

    LY = NZ - 1
    LX = LY + 2
    LP = LX + 1
    LM = LP + 1

    def tick(t):
        @pl.when(t < N)
        def _():
            begin(tok_copies(t, 0, True))

        @pl.when(t == 0)
        def _():
            for copy in w_copies[:4]:
                copy.start()

        @pl.when((t >= 1) & (t < NZ))
        def _():
            z_arrive(lambda k: metas.at[k], lambda way, k: m_recv.at[way, k], t)

            @pl.when(t < NZ - 1)
            def _():
                begin(meta_copies(t))

        def hop(d):
            f = t - d

            @pl.when((f >= 0) & (f < N))
            def _():
                z_arrive(lambda k: tokens.at[f, k], lambda way, k: z_recv.at[f, way, k], d)

                @pl.when(d < NZ - 1)
                def _():
                    begin(tok_copies(f, d))

        every(1, NZ, hop)

        @pl.when(t == LY)
        def _():
            choose()

        @pl.when((t >= LY) & (t < LY + N))
        def _():
            y_out(t - LY)

        @pl.when(t == LX)
        def _():
            for n in (0, 1):
                arrive(relay.at[n], w_recv.at[n])
                w_copies[4 + n].start()
            own_win.wait()

        @pl.when((t >= LX) & (t < LX + N))
        def _():
            x_out(t - LX)

        @pl.when((t >= LP) & (t < LP + N))
        def _():
            x_pass(t - LP)

        @pl.when((t >= LM) & (t < LM + N))
        def _():
            project(t - LM)

    every(0, LM + N, tick)

    gate_part = proj[:, :F]
    value = gate_part / (1.0 + jnp.exp(-gate_part)) * proj[:, F:]
    hid[x] = value.astype(jnp.bfloat16)
    HR = p.all_rows // 2

    def h_half(o, low):
        return hid.at[o, pl.ds(0 if low else HR, HR)]

    def h_copy(n):
        o, low, to = (
            (x, True, right), (x, False, left), (x, False, right), (x, True, left), (left, True, right), (right, False, left)
        )[n]
        return remote(h_half(o, low), h_half(o, low), h_send.at[n], h_recv.at[n], {"tensor": to})

    def h_arrive(n):
        o, low = ((left, True), (right, False), (left, False), (right, True), (across, True), (across, False))[n]
        arrive(h_half(o, low), h_recv.at[n])

    for n in range(4):
        h_copy(n).start()
    weigh()
    h_arrive(0)
    h_copy(4).start()
    h_arrive(1)
    h_copy(5).start()
    arrive(wcols.at[left], w_recv.at[2])
    arrive(wcols.at[right], w_recv.at[3])
    arrive(wcols.at[across, pl.ds(0, FH)], w_recv.at[4])
    arrive(wcols.at[across, pl.ds(FH, FH)], w_recv.at[5])
    own_wcols.wait()
    for n in range(2, 6):
        h_arrive(n)

    def b_copy(f, j):
        k = (y + j) % NY
        return remote(result.at[f, k], back.at[f, y], b_send.at[f, j], b_recv.at[f, j], at_y(k))

    def expand(f):
        total = jnp.zeros((p.all_rows, C), jnp.float32)
        for o in range(4):
            total = total + jnp.dot(
                hid[o], wcols[o, :, f * C : (f + 1) * C], preferred_element_type=jnp.float32
            )
        result[f] = total.astype(jnp.bfloat16).reshape(NY, p.rows, C)
        for j in range(1, NY):
            b_copy(f, j).start()
        back[f, y] = result[f, y]

    for f in range(N):
        expand(f)

    def combine(f):
        for j in range(1, NY):
            arrive(back.at[f, (y - j + NY) % NY], b_recv.at[f, j])
        value = jnp.dot(selgt[...], back[f].reshape(p.all_rows, C), preferred_element_type=jnp.float32)
        part[f] = value.reshape(NZ, T, C)

    def place_of(way):
        return z + way * (NZ - 1 - 2 * z)

    def c_copy(f, way, d):
        step = 1 - 2 * way
        to = z + step * d
        return remote(
            passed.at[way, f, to], carry.at[way, f, to], c_send.at[way, f, d], c_recv.at[way, f, d - 1], at_z(z + step)
        )

    def chain(f, way):
        place = place_of(way)

        def hop(i):
            d = NZ - 1 - i
            to = z + (1 - 2 * way) * d

            @pl.when(place + d < NZ)
            def _():
                @pl.when(place > 0)
                def _():
                    arrive(carry.at[way, f, to], c_recv.at[way, f, d])
                    passed[way, f, to] = (carry[way, f, to].astype(jnp.float32) + part[f, to]).astype(jnp.bfloat16)

                @pl.when(place == 0)
                def _():
                    passed[way, f, to] = part[f, to].astype(jnp.bfloat16)

                c_copy(f, way, d).start()

        every(0, NZ - 1, hop)

    def back_tick(t):
        @pl.when(t < N)
        def _():
            combine(t)

        for way in (0, 1):
            f = t - place_of(way)

            @pl.when((f >= 0) & (f < N))
            def _(f=f, way=way):
                chain(f, way)

    every(0, N + NZ - 1, back_tick)

    def finish(f):
        for way in (0, 1):
            @pl.when(place_of(way) > 0)
            def _(way=way):
                arrive(carry.at[way, f, z], c_recv.at[way, f, 0])
                part[f, z] = part[f, z] + carry[way, f, z].astype(jnp.float32)

        out_ref[:, f * C : (f + 1) * C] = part[f, z].astype(jnp.bfloat16)

    for f in range(N):
        finish(f)

    for j in range(1, NY):
        arrive(loads.at[(y - j + NY) % NY], l_recv.at[j])
    load_ref[...] = (jnp.sum(loads[...], axis=0) * p.scale)[0:1, : p.experts]

    left_all(meta_copies(0, True))
    every(1, NZ - 1, lambda d: left_all(meta_copies(d)))

    def settle(f):
        left_all(tok_copies(f, 0, True))
        every(1, NZ - 1, lambda d: left_all(tok_copies(f, d)))
        for j in range(1, NY):
            y_copy(f, j).wait_send()
            b_copy(f, j).wait_send()
        for n in range(6):
            x_copy(f, n).wait_send()
        for way in (0, 1):
            def gone(d, way=way):
                pl.when(place_of(way) + d < NZ)(c_copy(f, way, d).wait_send)

            every(1, NZ, gone)

    every(0, N, settle)
    for copy in w_copies:
        copy.wait_send()
    for n in range(6):
        h_copy(n).wait_send()
    for j in range(1, NY):
        load_copy(j).wait_send()


def shards(nz, ny, tokens, route_slots, route_scores, slot_expert, w_in, w_out):
    tok, width = tokens.shape
    top = route_slots.shape[1]
    _, full, _, hidden = w_in.shape
    slots = nz * ny
    experts = slots - slots // 4
    p = Plan(nz, ny, tok, top, width, hidden, experts, experts / (slots * tok * ROUTED))
    first = w_in.reshape(full, 2 * hidden)
    bf, f32 = jnp.bfloat16, jnp.float32
    dma = pltpu.SemaphoreType.DMA
    R, A, N, C, L = p.rows, p.all_rows, p.cuts, p.cut, nz * tok
    vmem = pl.BlockSpec(memory_space=pltpu.VMEM)
    smem = pl.BlockSpec(memory_space=pltpu.SMEM)
    anyspace = pl.BlockSpec(memory_space=pl.ANY)
    return pl.pallas_call(
        functools.partial(layer_kernel, p),
        out_shape=(
            jax.ShapeDtypeStruct((tok, width), bf),
            jax.ShapeDtypeStruct((1, experts), f32),
        ),
        in_specs=[vmem, vmem, vmem, smem, anyspace, anyspace],
        out_specs=(vmem, vmem),
        scratch_shapes=[
            pltpu.VMEM((2 * top, 2 * tok), f32),
            pltpu.VMEM((N, nz, tok, C), bf),
            pltpu.VMEM((nz, 2 * top, 2 * tok), f32),
            pltpu.VMEM((A, L), bf),
            pltpu.VMEM((A, L), f32),
            pltpu.VMEM((L, A), bf),
            pltpu.VMEM((N, ny, R, C), bf),
            pltpu.VMEM((4, N, ny, R, C), bf),
            pltpu.VMEM((A, 2 * hidden), f32),
            pltpu.VMEM((4, A, hidden), bf),
            pltpu.VMEM((4, hidden, width), bf),
            pltpu.VMEM((2, hidden // 2, width), bf),
            pltpu.VMEM((full, 2 * hidden), bf),
            pltpu.VMEM((N, ny, R, C), bf),
            pltpu.VMEM((N, ny, R, C), bf),
            pltpu.VMEM((N, nz, tok, C), f32),
            pltpu.VMEM((2, N, nz, tok, C), bf),
            pltpu.VMEM((2, N, nz, tok, C), bf),
            pltpu.VMEM((ny, 8, 128), f32),
            dma((N, 2, nz)), dma((N, 2, nz)),
            dma((2, nz)), dma((2, nz)),
            dma((N, ny)), dma((N, ny)),
            dma((N, 6)), dma((N, 6)),
            dma((6,)), dma((6,)),
            dma((6,)), dma((6,)),
            dma((N, ny)), dma((N, ny)),
            dma((2, N, nz)), dma((2, N, nz)),
            dma((ny,)), dma((ny,)),
            dma((2,)),
        ],
        compiler_params=pltpu.CompilerParams(
            collective_id=0, has_side_effects=True, vmem_limit_bytes=60 * 1024 * 1024
        ),
    )(tokens, route_slots.T, route_scores.T, slot_expert, first, w_out[0])


def solution(mesh, nz=8):
    ny = mesh.shape["expert"] // nz
    placed = (
        P(("dp", "expert"), "tensor"),
        P(("dp", "expert"), None),
        P(("dp", "expert"), None),
        P(),
        P("expert", None, None, "tensor"),
        P("expert", "tensor", None),
    )
    return jax.shard_map(
        functools.partial(shards, nz, ny),
        mesh=mesh,
        in_specs=placed,
        out_specs=(P(("dp", "expert"), "tensor"), P("dp", None)),
        check_vma=False,
    )
```

```python
import functools

import jax
import jax.numpy as jnp
from jax import lax
from jax.experimental import pallas as pl
from jax.experimental.pallas import tpu as pltpu
from jax.sharding import PartitionSpec as P

ROUTED = 2.5
MESH = pl.DeviceIdType.MESH


class Plan:
    def __init__(self, nz, ny, tok, top, width, hidden, experts, scale):
        self.nz, self.ny, self.tok, self.top = nz, ny, tok, top
        self.slots = nz * ny
        self.cap = 9 * tok * top // (8 * self.slots)
        self.rows = nz * self.cap
        self.all_rows = ny * self.rows
        self.width, self.hidden = width, hidden
        self.experts, self.scale = experts, scale
        self.cut = 128
        self.cuts = width // self.cut
        self.levels = nz.bit_length() - 1


def layer_kernel(
    p,
    tok_ref, slots_ref, scores_ref, held_ref, win_ref, wout_ref,
    out_ref, load_ref,
    tokens, metas, before, sel, selg, selgt, outgo, gath, proj, hid, wcols, relay, wraw, wfirst,
    result, back, part, carry, passed, carry_last, passed_last, loads,
    z_send, z_recv, m_send, m_recv, y_send, y_recv, x_send, x_recv,
    h_send, h_recv, w_send, w_recv, b_send, b_recv, c_send, c_recv, d_send, d_recv, l_send, l_recv, own,
):
    NZ, NY, T = p.nz, p.ny, p.tok
    W, F, C, N = p.width, p.hidden, p.cut, p.cuts
    L = NZ * T
    e = lax.axis_index("expert")
    x = lax.axis_index("tensor")
    z = e // NY
    y = e % NY
    right, left, across = (x + 1) % 4, (x + 3) % 4, (x + 2) % 4
    HY = NY // 2
    K = p.levels
    far = [NZ >> (k + 1) for k in range(K)]
    bits = [z // far[k] % 2 for k in range(K)]
    spot = sum(bits[k] * (1 << k) for k in range(K))
    mate = [z + far[k] * (1 - 2 * bits[k]) for k in range(K)]

    def line_place(r):
        return sum(r // (1 << k) % 2 * far[k] for k in range(K))


    def remote(src, dst, send, recv, dev):
        return pltpu.make_async_remote_copy(
            src_ref=src, dst_ref=dst, send_sem=send, recv_sem=recv, device_id=dev, device_id_type=MESH
        )

    def arrive(dst, recv):
        remote(dst, dst, recv, recv, {"tensor": right}).wait_recv()

    def at_z(k):
        return {"expert": k * NY + y}

    def at_y(k):
        return {"expert": z * NY + k}

    def every(lo, hi, body):
        def step(i, c):
            body(i)
            return c

        lax.fori_loop(lo, hi, step, 0)

    barrier = pltpu.get_barrier_semaphore()

    for j in range(1, NZ):
        pl.semaphore_signal(barrier, inc=1, device_id=at_z((z + j) % NZ), device_id_type=MESH)
    for j in range(1, NY):
        pl.semaphore_signal(barrier, inc=1, device_id=at_y((y + j) % NY), device_id_type=MESH)
    for n in (right, left):
        pl.semaphore_signal(barrier, inc=1, device_id={"tensor": n}, device_id_type=MESH)

    own_wcols = pltpu.make_async_copy(wout_ref.at[:, pl.ds(pl.multiple_of(x * W, 128), W)], wcols.at[x], own.at[0])
    own_win = pltpu.make_async_copy(win_ref, wraw, own.at[1])
    own_wcols.start()
    own_win.start()

    scores = scores_ref[...]
    gates = scores / jnp.sum(scores, axis=0, keepdims=True) * ROUTED
    names = slots_ref[...].astype(jnp.float32)
    for at in (0, T):
        metas[spot, : p.top, at : at + T] = names
        metas[spot, p.top :, at : at + T] = gates
    for f in range(N):
        tokens[f, spot] = tok_ref[:, f * C : (f + 1) * C]

    i0 = lax.broadcasted_iota(jnp.int32, (L, L), 0)
    i1 = lax.broadcasted_iota(jnp.int32, (L, L), 1)
    before[...] = jnp.where((i0 < i1) & (i0 // T == i1 // T), 1.0, 0.0).astype(jnp.bfloat16)
    proj[...] = jnp.zeros_like(proj)
    pl.semaphore_wait(barrier, NY - 1 + 2 + NZ - 1)

    def held_at(k):
        return pl.ds(spot // (1 << k) * (1 << k), 1 << k)

    def coming_at(k):
        return pl.ds(spot // (2 << k) * (2 << k) + (1 - bits[k]) * (1 << k), 1 << k)

    def meta_copy(j):
        ref = metas.at[spot]
        return remote(ref, ref, m_send.at[j], m_recv.at[j], at_z(line_place((spot + j) % NZ)))

    def tok_copy(f, k):
        ref = tokens.at[f, held_at(k)]
        return remote(ref, ref, z_send.at[f, k], z_recv.at[f, k], at_z(mate[k]))

    def wblock(k, r0, n):
        return wout_ref.at[pl.ds(r0, n), pl.ds(pl.multiple_of(k * W, 128), W)]

    FH = F // 2
    w_copies = [
        remote(wblock(across, 0, FH), relay.at[0], w_send.at[0], w_recv.at[0], {"tensor": right}),
        remote(wblock(across, FH, FH), relay.at[1], w_send.at[1], w_recv.at[1], {"tensor": left}),
        remote(wblock(right, 0, F), wcols.at[x], w_send.at[2], w_recv.at[2], {"tensor": right}),
        remote(wblock(left, 0, F), wcols.at[x], w_send.at[3], w_recv.at[3], {"tensor": left}),
        remote(relay.at[0], wcols.at[left, pl.ds(0, FH)], w_send.at[4], w_recv.at[4], {"tensor": right}),
        remote(relay.at[1], wcols.at[right, pl.ds(FH, FH)], w_send.at[5], w_recv.at[5], {"tensor": left}),
    ]

    def line_routes():
        lane = lax.broadcasted_iota(jnp.int32, (p.top, 2 * T), 1)
        slots, gates = [], []
        for k in range(0, NZ, 2):
            a, b = metas[k], metas[k + 1]
            slots.append(jnp.where(lane < T, a[: p.top], b[: p.top]))
            gates.append(jnp.where(lane < T, a[p.top :], b[p.top :]))
        return jnp.concatenate(slots, axis=1).astype(jnp.int32), jnp.concatenate(gates, axis=1)

    def choose():
        slots, gates = line_routes()
        mine = lax.broadcasted_iota(jnp.int32, (NY, L), 0) + z * NY
        match = jnp.zeros((NY, L), jnp.float32)
        gate = jnp.zeros((NY, L), jnp.float32)
        for k in range(p.top):
            eq = slots[k : k + 1] == mine
            match = match + jnp.where(eq, 1.0, 0.0)
            gate = gate + jnp.where(eq, gates[k : k + 1], 0.0)
        rank = jnp.dot(match.astype(jnp.bfloat16), before[...], preferred_element_type=jnp.float32)
        block = lax.broadcasted_iota(jnp.int32, (NY, L), 1) // T
        key = jnp.where(match > 0.5, rank.astype(jnp.int32) * NZ + block, -1)
        place = lax.broadcasted_iota(jnp.int32, (p.rows, L), 0)
        for k in range(NY):
            hit = key[k : k + 1] == place
            rows = pl.ds(k * p.rows, p.rows)
            sel[rows] = jnp.where(hit, 1.0, 0.0).astype(jnp.bfloat16)
            selg[rows] = jnp.where(hit, gate[k : k + 1], 0.0)

    def load_copy(j):
        return remote(loads.at[y], loads.at[y], l_send.at[j], l_recv.at[j], at_y((y + j) % NY))

    def weigh():
        slots, gates = line_routes()
        names = lax.broadcasted_iota(jnp.int32, (p.slots, L), 0)
        total = jnp.zeros((p.slots, L), jnp.float32)
        for k in range(p.top):
            total = total + jnp.where(slots[k : k + 1] == names, gates[k : k + 1], 0.0)
        total = jnp.broadcast_to(jnp.sum(total, axis=1, keepdims=True), (p.slots, 128))
        expert = lax.broadcasted_iota(jnp.int32, (1, 128), 1)
        row = jnp.zeros((1, 128), jnp.float32)
        for s in range(p.slots):
            row = row + jnp.where(expert == held_ref[s], total[s : s + 1], 0.0)
        loads[y] = jnp.broadcast_to(row, (8, 128))
        for j in range(1, NY):
            load_copy(j).start()
        selgt[...] = jnp.transpose(selg[...], (1, 0)).astype(jnp.bfloat16)

    def y_copy(f, j):
        k = (y + j) % NY
        return remote(outgo.at[f, k], gath.at[x, f, y], y_send.at[f, j], y_recv.at[f, j], at_y(k))

    def y_out(f):
        rows = jnp.dot(sel[...], tokens[f].reshape(L, C), preferred_element_type=jnp.float32)
        outgo[f] = rows.astype(jnp.bfloat16).reshape(NY, p.rows, C)
        for j in range(1, NY):
            y_copy(f, j).start()
        gath[x, f, y] = outgo[f, y]

    def half(o, f, low):
        return gath.at[o, f, pl.ds(0 if low else HY, HY)]

    def x_copy(f, n):
        o, low, to = (
            (x, True, right), (x, False, left), (x, False, right), (x, True, left), (left, True, right), (right, False, left)
        )[n]
        return remote(half(o, f, low), half(o, f, low), x_send.at[f, n], x_recv.at[f, n], {"tensor": to})

    def x_arrive(f, n):
        o, low = ((left, True), (right, False), (left, False), (right, True), (across, True), (across, False))[n]
        arrive(half(o, f, low), x_recv.at[f, n])

    def x_out(f):
        for j in range(1, NY):
            arrive(gath.at[x, f, (y - j + NY) % NY], y_recv.at[f, j])
        for n in range(4):
            x_copy(f, n).start()

    def x_pass(f):
        x_arrive(f, 0)
        x_copy(f, 4).start()
        x_arrive(f, 1)
        x_copy(f, 5).start()

    def project(f):
        for n in range(2, 6):
            x_arrive(f, n)

        def add_up(first, n):
            total = proj[...]
            for o in range(4):
                rows = [gath[o, first + i].reshape(p.all_rows, C) for i in range(n)]
                total = total + jnp.dot(
                    rows[0] if n == 1 else jnp.concatenate(rows, axis=1),
                    wfirst[pl.ds(pl.multiple_of(o * W + first * C, C), n * C), :],
                    preferred_element_type=jnp.float32,
                )
            proj[...] = total

        pl.when(f % 2 == 1)(lambda: add_up(f - 1, 2))
        if N % 2:
            pl.when(f == N - 1)(lambda: add_up(f, 1))

    def tell_apart(i):
        def part_of(j):
            r0 = pl.multiple_of((i * 4 + j) * C, C)
            pairs = wraw[pl.ds(r0, C)].reshape(2 * C, F)
            row = lax.broadcasted_iota(jnp.int32, (C, 2 * C), 0)
            col = lax.broadcasted_iota(jnp.int32, (C, 2 * C), 1)
            for g in (0, 1):
                pick = jnp.where(col == 2 * row + g, 1.0, 0.0).astype(jnp.bfloat16)
                got = jnp.dot(pick, pairs, preferred_element_type=jnp.float32)
                wfirst[pl.ds(r0, C), g * F : (g + 1) * F] = got.astype(jnp.bfloat16)

        every(0, 4, part_of)

    for j in range(1, NZ):
        meta_copy(j).start()
    own_win.wait()

    LZ = [2 * k for k in range(K)]
    LY = LZ[-1] + 2
    LX = LY + 2
    LP = LX + 1
    LM = LP + 1

    def tick(t):
        for k in range(K):
            @pl.when((t >= LZ[k]) & (t < LZ[k] + N))
            def _(k=k):
                f = t - LZ[k]
                if k:
                    arrive(tokens.at[f, coming_at(k - 1)], z_recv.at[f, k - 1])
                tok_copy(f, k).start()

        @pl.when(t == 1)
        def _():
            for copy in w_copies[:4]:
                copy.start()

        @pl.when(t < 5)
        def _():
            every(jnp.where(t < 2, 2 * t, t + 2), jnp.minimum(jnp.where(t < 2, 2 * t + 2, t + 3), N), tell_apart)

        @pl.when(t == LY - 1)
        def _():
            for j in range(1, NZ):
                arrive(metas.at[(spot - j + NZ) % NZ], m_recv.at[j])
            choose()

        @pl.when((t >= LY) & (t < LY + N))
        def _():
            arrive(tokens.at[t - LY, coming_at(K - 1)], z_recv.at[t - LY, K - 1])
            y_out(t - LY)

        @pl.when(t == LX)
        def _():
            for n in (0, 1):
                arrive(relay.at[n], w_recv.at[n])
                w_copies[4 + n].start()

        @pl.when((t >= LX) & (t < LX + N))
        def _():
            x_out(t - LX)

        @pl.when((t >= LP) & (t < LP + N))
        def _():
            x_pass(t - LP)

        @pl.when((t >= LM) & (t < LM + N))
        def _():
            project(t - LM)

    every(0, LM + N, tick)

    gate_part = proj[:, :F]
    value = gate_part / (1.0 + jnp.exp(-gate_part)) * proj[:, F:]
    hid[x] = value.astype(jnp.bfloat16)
    HR = p.all_rows // 2

    def h_half(o, low):
        return hid.at[o, pl.ds(0 if low else HR, HR)]

    def h_copy(n):
        o, low, to = (
            (x, True, right), (x, False, left), (x, False, right), (x, True, left), (left, True, right), (right, False, left)
        )[n]
        return remote(h_half(o, low), h_half(o, low), h_send.at[n], h_recv.at[n], {"tensor": to})

    def h_arrive(n):
        o, low = ((left, True), (right, False), (left, False), (right, True), (across, True), (across, False))[n]
        arrive(h_half(o, low), h_recv.at[n])

    for n in range(4):
        h_copy(n).start()
    weigh()
    h_arrive(0)
    h_copy(4).start()
    h_arrive(1)
    h_copy(5).start()
    arrive(wcols.at[left], w_recv.at[2])
    arrive(wcols.at[right], w_recv.at[3])
    arrive(wcols.at[across, pl.ds(0, FH)], w_recv.at[4])
    arrive(wcols.at[across, pl.ds(FH, FH)], w_recv.at[5])
    own_wcols.wait()
    for n in range(2, 6):
        h_arrive(n)

    def b_copy(f, j):
        k = (y + j) % NY
        return remote(result.at[f, k], back.at[f, y], b_send.at[f, j], b_recv.at[f, j], at_y(k))

    def expand(first, n):
        total = jnp.zeros((p.all_rows, n * C), jnp.float32)
        for o in range(4):
            total = total + jnp.dot(
                hid[o], wcols[o, :, first * C : (first + n) * C], preferred_element_type=jnp.float32
            )
        total = total.astype(jnp.bfloat16)
        for i in range(n):
            f = first + i
            result[f] = total[:, i * C : (i + 1) * C].reshape(NY, p.rows, C)
            for j in range(1, NY):
                b_copy(f, j).start()
            back[f, y] = result[f, y]

    if N % 2:
        expand(0, 1)
    for f in range(N % 2, N, 2):
        expand(f, 2)

    def combine(f):
        for j in range(1, NY):
            arrive(back.at[f, (y - j + NY) % NY], b_recv.at[f, j])
        value = jnp.dot(selgt[...], back[f].reshape(p.all_rows, C), preferred_element_type=jnp.float32)
        part[f] = value.reshape(NZ, T, C)
        pl.when(f < N - 1)(lambda: pass_on(f, K - 1))

        @pl.when(f == N - 1)
        def _():
            passed_last[...] = part[f].astype(jnp.bfloat16)
            for j in range(1, NZ):
                d_copy(j).start()

    def d_copy(j):
        to = (spot + j) % NZ
        return remote(passed_last.at[to], carry_last.at[spot], d_send.at[j], d_recv.at[j], at_z(line_place(to)))

    def last_in():
        total = part[N - 1, spot]
        for j in range(1, NZ):
            k = (spot - j + NZ) % NZ
            arrive(carry_last.at[k], d_recv.at[j])
            total = total + carry_last[k].astype(jnp.float32)
        out_ref[:, (N - 1) * C :] = total.astype(jnp.bfloat16)

    def c_copy(f, k):
        ref = pl.ds(1 << k, 1 << k)
        return remote(passed.at[f, ref], carry.at[f, ref], c_send.at[f, k], c_recv.at[f, k], at_z(mate[k]))

    def pass_on(f, k):
        passed[f, (1 << k) : (2 << k)] = part[f, coming_at(k)].astype(jnp.bfloat16)
        c_copy(f, k).start()

    def take_in(f, k):
        arrive(carry.at[f, pl.ds(1 << k, 1 << k)], c_recv.at[f, k])
        total = part[f, held_at(k)] + carry[f, (1 << k) : (2 << k)].astype(jnp.float32)
        if k:
            part[f, held_at(k)] = total
            pass_on(f, k - 1)
        else:
            out_ref[:, pl.ds(pl.multiple_of(f * C, C), C)] = total[0].astype(jnp.bfloat16)

    def back_tick(t):
        @pl.when(t < N)
        def _():
            combine(t)

        for i in range(K):
            @pl.when((t >= 2 * i + 2) & (t < 2 * i + 1 + N))
            def _(i=i):
                take_in(t - 2 * i - 2, K - 1 - i)

    every(0, 2 * K + N - 1, back_tick)
    last_in()

    for j in range(1, NY):
        arrive(loads.at[(y - j + NY) % NY], l_recv.at[j])
    load_ref[...] = (jnp.sum(loads[...], axis=0) * p.scale)[0:1, : p.experts]

    for j in range(1, NZ):
        meta_copy(j).wait_send()
        d_copy(j).wait_send()

    def settle(f):
        for k in range(K):
            tok_copy(f, k).wait_send()
            pl.when(f < N - 1)(c_copy(f, k).wait_send)
        for j in range(1, NY):
            y_copy(f, j).wait_send()
            b_copy(f, j).wait_send()
        for n in range(6):
            x_copy(f, n).wait_send()

    every(0, N, settle)
    for copy in w_copies:
        copy.wait_send()
    for n in range(6):
        h_copy(n).wait_send()
    for j in range(1, NY):
        load_copy(j).wait_send()


def shards(nz, ny, tokens, route_slots, route_scores, slot_expert, w_in, w_out):
    tok, width = tokens.shape
    top = route_slots.shape[1]
    _, full, _, hidden = w_in.shape
    slots = nz * ny
    experts = slots - slots // 4
    p = Plan(nz, ny, tok, top, width, hidden, experts, experts / (slots * tok * ROUTED))
    bf, f32 = jnp.bfloat16, jnp.float32
    dma = pltpu.SemaphoreType.DMA
    R, A, N, C, L = p.rows, p.all_rows, p.cuts, p.cut, nz * tok
    vmem = pl.BlockSpec(memory_space=pltpu.VMEM)
    smem = pl.BlockSpec(memory_space=pltpu.SMEM)
    anyspace = pl.BlockSpec(memory_space=pl.ANY)
    return pl.pallas_call(
        functools.partial(layer_kernel, p),
        out_shape=(
            jax.ShapeDtypeStruct((tok, width), bf),
            jax.ShapeDtypeStruct((1, experts), f32),
        ),
        in_specs=[vmem, vmem, vmem, smem, anyspace, anyspace],
        out_specs=(vmem, vmem),
        scratch_shapes=[
            pltpu.VMEM((N, nz, tok, C), bf),
            pltpu.VMEM((nz, 2 * top, 2 * tok), f32),
            pltpu.VMEM((L, L), bf),
            pltpu.VMEM((A, L), bf),
            pltpu.VMEM((A, L), f32),
            pltpu.VMEM((L, A), bf),
            pltpu.VMEM((N, ny, R, C), bf),
            pltpu.VMEM((4, N, ny, R, C), bf),
            pltpu.VMEM((A, 2 * hidden), f32),
            pltpu.VMEM((4, A, hidden), bf),
            pltpu.VMEM((4, hidden, width), bf),
            pltpu.VMEM((2, hidden // 2, width), bf),
            pltpu.VMEM((full, 2, hidden), bf),
            pltpu.VMEM((full, 2 * hidden), bf),
            pltpu.VMEM((N, ny, R, C), bf),
            pltpu.VMEM((N, ny, R, C), bf),
            pltpu.VMEM((N, nz, tok, C), f32),
            pltpu.VMEM((N, nz, tok, C), bf),
            pltpu.VMEM((N, nz, tok, C), bf),
            pltpu.VMEM((nz, tok, C), bf),
            pltpu.VMEM((nz, tok, C), bf),
            pltpu.VMEM((ny, 8, 128), f32),
            dma((N, p.levels)), dma((N, p.levels)),
            dma((nz,)), dma((nz,)),
            dma((N, ny)), dma((N, ny)),
            dma((N, 6)), dma((N, 6)),
            dma((6,)), dma((6,)),
            dma((6,)), dma((6,)),
            dma((N, ny)), dma((N, ny)),
            dma((N, p.levels)), dma((N, p.levels)),
            dma((nz,)), dma((nz,)),
            dma((ny,)), dma((ny,)),
            dma((2,)),
        ],
        compiler_params=pltpu.CompilerParams(
            collective_id=0, has_side_effects=True, vmem_limit_bytes=60 * 1024 * 1024
        ),
    )(tokens, route_slots.T, route_scores.T, slot_expert, w_in[0], w_out[0])


def solution(mesh, nz=8):
    ny = mesh.shape["expert"] // nz
    placed = (
        P(("dp", "expert"), "tensor"),
        P(("dp", "expert"), None),
        P(("dp", "expert"), None),
        P(),
        P("expert", None, None, "tensor"),
        P("expert", "tensor", None),
    )
    return jax.shard_map(
        functools.partial(shards, nz, ny),
        mesh=mesh,
        in_specs=placed,
        out_specs=(P(("dp", "expert"), "tensor"), P("dp", None)),
        check_vma=False,
    )
```

```python
import functools

import jax
import jax.numpy as jnp
from jax import lax
from jax.experimental import pallas as pl
from jax.experimental.pallas import tpu as pltpu
from jax.sharding import PartitionSpec as P

ROUTED = 2.5
MESH = pl.DeviceIdType.MESH


class Plan:
    def __init__(self, nz, ny, tok, top, width, hidden, experts, scale):
        self.nz, self.ny, self.tok, self.top = nz, ny, tok, top
        self.slots = nz * ny
        self.cap = 9 * tok * top // (8 * self.slots)
        self.rows = nz * self.cap
        self.all_rows = ny * self.rows
        self.width, self.hidden = width, hidden
        self.experts, self.scale = experts, scale
        self.cut = 128
        self.cuts = width // self.cut
        self.levels = nz.bit_length() - 1


def layer_kernel(
    p,
    tok_ref, slots_ref, scores_ref, held_ref, win_ref, wout_ref,
    out_ref, load_ref,
    tokens, metas, before, sel, selg, selgt, outgo, gath, proj, hid, wcols, relay, wraw, wfirst,
    result, back, part, carry, passed, carry_last, passed_last, loads,
    z_send, z_recv, m_send, m_recv, y_send, y_recv, x_send, x_recv,
    h_send, h_recv, w_send, w_recv, b_send, b_recv, c_send, c_recv, d_send, d_recv, f_send, f_recv, l_send, l_recv, own,
):
    NZ, NY, T = p.nz, p.ny, p.tok
    W, F, C, N = p.width, p.hidden, p.cut, p.cuts
    L = NZ * T
    e = lax.axis_index("expert")
    x = lax.axis_index("tensor")
    z = e // NY
    y = e % NY
    right, left, across = (x + 1) % 4, (x + 3) % 4, (x + 2) % 4
    HY = NY // 2
    K = p.levels
    far = [NZ >> (k + 1) for k in range(K)]
    bits = [z // far[k] % 2 for k in range(K)]
    spot = sum(bits[k] * (1 << k) for k in range(K))
    mate = [z + far[k] * (1 - 2 * bits[k]) for k in range(K)]

    def line_place(r):
        return sum(r // (1 << k) % 2 * far[k] for k in range(K))


    def remote(src, dst, send, recv, dev):
        return pltpu.make_async_remote_copy(
            src_ref=src, dst_ref=dst, send_sem=send, recv_sem=recv, device_id=dev, device_id_type=MESH
        )

    def arrive(dst, recv):
        remote(dst, dst, recv, recv, {"tensor": right}).wait_recv()

    def at_z(k):
        return {"expert": k * NY + y}

    def at_y(k):
        return {"expert": z * NY + k}

    def every(lo, hi, body):
        def step(i, c):
            body(i)
            return c

        lax.fori_loop(lo, hi, step, 0)

    barrier = pltpu.get_barrier_semaphore()

    for j in range(1, NZ):
        pl.semaphore_signal(barrier, inc=1, device_id=at_z((z + j) % NZ), device_id_type=MESH)
    for j in range(1, NY):
        pl.semaphore_signal(barrier, inc=1, device_id=at_y((y + j) % NY), device_id_type=MESH)
    for n in (right, left):
        pl.semaphore_signal(barrier, inc=1, device_id={"tensor": n}, device_id_type=MESH)

    own_wcols = pltpu.make_async_copy(wout_ref.at[:, pl.ds(pl.multiple_of(x * W, 128), W)], wcols.at[x], own.at[0])
    own_win = pltpu.make_async_copy(win_ref, wraw, own.at[1])
    own_wcols.start()
    own_win.start()

    scores = scores_ref[...]
    gates = scores / jnp.sum(scores, axis=0, keepdims=True) * ROUTED
    names = slots_ref[...].astype(jnp.float32)
    for at in (0, T):
        metas[spot, : p.top, at : at + T] = names
        metas[spot, p.top :, at : at + T] = gates
    for f in range(N):
        tokens[f, spot] = tok_ref[:, f * C : (f + 1) * C]

    i0 = lax.broadcasted_iota(jnp.int32, (L, L), 0)
    i1 = lax.broadcasted_iota(jnp.int32, (L, L), 1)
    before[...] = jnp.where((i0 < i1) & (i0 // T == i1 // T), 1.0, 0.0).astype(jnp.bfloat16)
    proj[...] = jnp.zeros_like(proj)
    pl.semaphore_wait(barrier, NY - 1 + 2 + NZ - 1)

    def held_at(k):
        return pl.ds(spot // (1 << k) * (1 << k), 1 << k)

    def coming_at(k):
        return pl.ds(spot // (2 << k) * (2 << k) + (1 - bits[k]) * (1 << k), 1 << k)

    def meta_copy(j):
        ref = metas.at[spot]
        return remote(ref, ref, m_send.at[j], m_recv.at[j], at_z(line_place((spot + j) % NZ)))

    def first_copy(j):
        ref = tokens.at[0, spot]
        return remote(ref, ref, f_send.at[j], f_recv.at[j], at_z(line_place((spot + j) % NZ)))

    def tok_copy(f, k):
        ref = tokens.at[f, held_at(k)]
        return remote(ref, ref, z_send.at[f, k], z_recv.at[f, k], at_z(mate[k]))

    def wblock(k, r0, n):
        return wout_ref.at[pl.ds(r0, n), pl.ds(pl.multiple_of(k * W, 128), W)]

    FH = F // 2
    w_copies = [
        remote(wblock(across, 0, FH), relay.at[0], w_send.at[0], w_recv.at[0], {"tensor": right}),
        remote(wblock(across, FH, FH), relay.at[1], w_send.at[1], w_recv.at[1], {"tensor": left}),
        remote(wblock(right, 0, F), wcols.at[x], w_send.at[2], w_recv.at[2], {"tensor": right}),
        remote(wblock(left, 0, F), wcols.at[x], w_send.at[3], w_recv.at[3], {"tensor": left}),
        remote(relay.at[0], wcols.at[left, pl.ds(0, FH)], w_send.at[4], w_recv.at[4], {"tensor": right}),
        remote(relay.at[1], wcols.at[right, pl.ds(FH, FH)], w_send.at[5], w_recv.at[5], {"tensor": left}),
    ]

    def line_routes():
        lane = lax.broadcasted_iota(jnp.int32, (p.top, 2 * T), 1)
        slots, gates = [], []
        for k in range(0, NZ, 2):
            a, b = metas[k], metas[k + 1]
            slots.append(jnp.where(lane < T, a[: p.top], b[: p.top]))
            gates.append(jnp.where(lane < T, a[p.top :], b[p.top :]))
        return jnp.concatenate(slots, axis=1).astype(jnp.int32), jnp.concatenate(gates, axis=1)

    def choose():
        slots, gates = line_routes()
        mine = lax.broadcasted_iota(jnp.int32, (NY, L), 0) + z * NY
        match = jnp.zeros((NY, L), jnp.float32)
        gate = jnp.zeros((NY, L), jnp.float32)
        for k in range(p.top):
            eq = slots[k : k + 1] == mine
            match = match + jnp.where(eq, 1.0, 0.0)
            gate = gate + jnp.where(eq, gates[k : k + 1], 0.0)
        rank = jnp.dot(match.astype(jnp.bfloat16), before[...], preferred_element_type=jnp.float32)
        block = lax.broadcasted_iota(jnp.int32, (NY, L), 1) // T
        key = jnp.where(match > 0.5, rank.astype(jnp.int32) * NZ + block, -1)
        place = lax.broadcasted_iota(jnp.int32, (p.rows, L), 0)
        for k in range(NY):
            hit = key[k : k + 1] == place
            rows = pl.ds(k * p.rows, p.rows)
            sel[rows] = jnp.where(hit, 1.0, 0.0).astype(jnp.bfloat16)
            selg[rows] = jnp.where(hit, gate[k : k + 1], 0.0)

    def load_copy(j):
        return remote(loads.at[y], loads.at[y], l_send.at[j], l_recv.at[j], at_y((y + j) % NY))

    def weigh():
        slots, gates = line_routes()
        names = lax.broadcasted_iota(jnp.int32, (p.slots, L), 0)
        total = jnp.zeros((p.slots, L), jnp.float32)
        for k in range(p.top):
            total = total + jnp.where(slots[k : k + 1] == names, gates[k : k + 1], 0.0)
        total = jnp.broadcast_to(jnp.sum(total, axis=1, keepdims=True), (p.slots, 128))
        expert = lax.broadcasted_iota(jnp.int32, (1, 128), 1)
        row = jnp.zeros((1, 128), jnp.float32)
        for s in range(p.slots):
            row = row + jnp.where(expert == held_ref[s], total[s : s + 1], 0.0)
        loads[y] = jnp.broadcast_to(row, (8, 128))
        for j in range(1, NY):
            load_copy(j).start()
        selgt[...] = jnp.transpose(selg[...], (1, 0)).astype(jnp.bfloat16)

    def y_copy(f, j):
        k = (y + j) % NY
        return remote(outgo.at[f, k], gath.at[x, f, y], y_send.at[f, j], y_recv.at[f, j], at_y(k))

    def y_out(f):
        rows = jnp.dot(sel[...], tokens[f].reshape(L, C), preferred_element_type=jnp.float32)
        outgo[f] = rows.astype(jnp.bfloat16).reshape(NY, p.rows, C)
        for j in range(1, NY):
            y_copy(f, j).start()
        gath[x, f, y] = outgo[f, y]

    def half(o, f, low):
        return gath.at[o, f, pl.ds(0 if low else HY, HY)]

    def x_copy(f, n):
        o, low, to = (
            (x, True, right), (x, False, left), (x, False, right), (x, True, left), (left, True, right), (right, False, left)
        )[n]
        return remote(half(o, f, low), half(o, f, low), x_send.at[f, n], x_recv.at[f, n], {"tensor": to})

    def x_arrive(f, n):
        o, low = ((left, True), (right, False), (left, False), (right, True), (across, True), (across, False))[n]
        arrive(half(o, f, low), x_recv.at[f, n])

    def x_out(f):
        for j in range(1, NY):
            arrive(gath.at[x, f, (y - j + NY) % NY], y_recv.at[f, j])
        for n in range(4):
            x_copy(f, n).start()

    def x_pass(f):
        x_arrive(f, 0)
        x_copy(f, 4).start()
        x_arrive(f, 1)
        x_copy(f, 5).start()

    def project(f):
        for n in range(2, 6):
            x_arrive(f, n)

        def add_up(first, n):
            total = proj[...]
            for o in range(4):
                rows = [gath[o, first + i].reshape(p.all_rows, C) for i in range(n)]
                total = total + jnp.dot(
                    rows[0] if n == 1 else jnp.concatenate(rows, axis=1),
                    wfirst[pl.ds(pl.multiple_of(o * W + first * C, C), n * C), :],
                    preferred_element_type=jnp.float32,
                )
            proj[...] = total

        pl.when(f % 2 == 1)(lambda: add_up(f - 1, 2))
        if N % 2:
            pl.when(f == N - 1)(lambda: add_up(f, 1))

    def tell_apart(i):
        def part_of(j):
            r0 = pl.multiple_of((i * 4 + j) * C, C)
            pairs = wraw[pl.ds(r0, C)].reshape(2 * C, F)
            row = lax.broadcasted_iota(jnp.int32, (C, 2 * C), 0)
            col = lax.broadcasted_iota(jnp.int32, (C, 2 * C), 1)
            for g in (0, 1):
                pick = jnp.where(col == 2 * row + g, 1.0, 0.0).astype(jnp.bfloat16)
                got = jnp.dot(pick, pairs, preferred_element_type=jnp.float32)
                wfirst[pl.ds(r0, C), g * F : (g + 1) * F] = got.astype(jnp.bfloat16)

        every(0, 4, part_of)

    for j in range(1, NZ):
        meta_copy(j).start()
    for j in range(1, NZ):
        first_copy(j).start()
    for f in range(1, N):
        tok_copy(f, 0).start()
    for copy in w_copies[:4]:
        copy.start()
    own_win.wait()
    every(0, min(3, N), tell_apart)
    for j in range(1, NZ):
        arrive(metas.at[(spot - j + NZ) % NZ], m_recv.at[j])
    choose()
    for j in range(1, NZ):
        arrive(tokens.at[0, (spot - j + NZ) % NZ], f_recv.at[j])
    y_out(0)

    LZ = [2 * k - 3 for k in range(K)]
    LY = LZ[-1] + 2
    LX = LY + 2
    LP = LX + 1
    LM = LP + 1

    def tick(t):
        for k in range(1, K):
            @pl.when((t >= LZ[k] + 1) & (t < LZ[k] + N))
            def _(k=k):
                f = t - LZ[k]
                arrive(tokens.at[f, coming_at(k - 1)], z_recv.at[f, k - 1])
                tok_copy(f, k).start()

        @pl.when(t + 3 < N)
        def _():
            tell_apart(t + 3)

        @pl.when((t >= LY + 1) & (t < LY + N))
        def _():
            arrive(tokens.at[t - LY, coming_at(K - 1)], z_recv.at[t - LY, K - 1])
            y_out(t - LY)

        pl.when(t == 2)(lambda: x_out(0))
        pl.when(t == 4)(lambda: x_pass(0))

        @pl.when(t == LX)
        def _():
            for n in (0, 1):
                arrive(relay.at[n], w_recv.at[n])
                w_copies[4 + n].start()

        @pl.when((t >= LX + 1) & (t < LX + N))
        def _():
            x_out(t - LX)

        @pl.when((t >= LP + 1) & (t < LP + N))
        def _():
            x_pass(t - LP)

        @pl.when((t >= LM) & (t < LM + N))
        def _():
            project(t - LM)

    every(0, LM + N, tick)

    gate_part = proj[:, :F]
    value = gate_part / (1.0 + jnp.exp(-gate_part)) * proj[:, F:]
    hid[x] = value.astype(jnp.bfloat16)
    HR = p.all_rows // 2

    def h_half(o, low):
        return hid.at[o, pl.ds(0 if low else HR, HR)]

    def h_copy(n):
        o, low, to = (
            (x, True, right), (x, False, left), (x, False, right), (x, True, left), (left, True, right), (right, False, left)
        )[n]
        return remote(h_half(o, low), h_half(o, low), h_send.at[n], h_recv.at[n], {"tensor": to})

    def h_arrive(n):
        o, low = ((left, True), (right, False), (left, False), (right, True), (across, True), (across, False))[n]
        arrive(h_half(o, low), h_recv.at[n])

    for n in range(4):
        h_copy(n).start()
    h_arrive(0)
    h_copy(4).start()
    h_arrive(1)
    h_copy(5).start()
    weigh()
    arrive(wcols.at[left], w_recv.at[2])
    arrive(wcols.at[right], w_recv.at[3])
    arrive(wcols.at[across, pl.ds(0, FH)], w_recv.at[4])
    arrive(wcols.at[across, pl.ds(FH, FH)], w_recv.at[5])
    own_wcols.wait()
    for n in range(2, 6):
        h_arrive(n)

    def b_copy(f, j):
        k = (y + j) % NY
        return remote(result.at[f, k], back.at[f, y], b_send.at[f, j], b_recv.at[f, j], at_y(k))

    def expand(first, n):
        total = jnp.zeros((p.all_rows, n * C), jnp.float32)
        for o in range(4):
            total = total + jnp.dot(
                hid[o], wcols[o, :, first * C : (first + n) * C], preferred_element_type=jnp.float32
            )
        total = total.astype(jnp.bfloat16)
        for i in range(n):
            f = first + i
            result[f] = total[:, i * C : (i + 1) * C].reshape(NY, p.rows, C)
            for j in range(1, NY):
                b_copy(f, j).start()
            back[f, y] = result[f, y]

    if N % 2:
        expand(0, 1)
    for f in range(N % 2, N, 2):
        expand(f, 2)

    def combine(f):
        for j in range(1, NY):
            arrive(back.at[f, (y - j + NY) % NY], b_recv.at[f, j])
        value = jnp.dot(selgt[...], back[f].reshape(p.all_rows, C), preferred_element_type=jnp.float32)
        part[f] = value.reshape(NZ, T, C)
        pl.when(f < N - 1)(lambda: pass_on(f, K - 1))

        @pl.when(f == N - 1)
        def _():
            passed_last[...] = part[f].astype(jnp.bfloat16)
            for j in range(1, NZ):
                d_copy(j).start()

    def d_copy(j):
        to = (spot + j) % NZ
        return remote(passed_last.at[to], carry_last.at[spot], d_send.at[j], d_recv.at[j], at_z(line_place(to)))

    def last_in():
        total = part[N - 1, spot]
        for j in range(1, NZ):
            k = (spot - j + NZ) % NZ
            arrive(carry_last.at[k], d_recv.at[j])
            total = total + carry_last[k].astype(jnp.float32)
        out_ref[:, (N - 1) * C :] = total.astype(jnp.bfloat16)

    def c_copy(f, k):
        ref = pl.ds(1 << k, 1 << k)
        return remote(passed.at[f, ref], carry.at[f, ref], c_send.at[f, k], c_recv.at[f, k], at_z(mate[k]))

    def pass_on(f, k):
        passed[f, (1 << k) : (2 << k)] = part[f, coming_at(k)].astype(jnp.bfloat16)
        c_copy(f, k).start()

    def take_in(f, k):
        arrive(carry.at[f, pl.ds(1 << k, 1 << k)], c_recv.at[f, k])
        total = part[f, held_at(k)] + carry[f, (1 << k) : (2 << k)].astype(jnp.float32)
        if k:
            part[f, held_at(k)] = total
            pass_on(f, k - 1)
        else:
            out_ref[:, pl.ds(pl.multiple_of(f * C, C), C)] = total[0].astype(jnp.bfloat16)

    def back_tick(t):
        @pl.when(t < N)
        def _():
            combine(t)

        for i in range(K):
            @pl.when((t >= 2 * i + 2) & (t < 2 * i + 1 + N))
            def _(i=i):
                take_in(t - 2 * i - 2, K - 1 - i)

    every(0, 2 * K + N - 1, back_tick)
    last_in()

    for j in range(1, NY):
        arrive(loads.at[(y - j + NY) % NY], l_recv.at[j])
    load_ref[...] = (jnp.sum(loads[...], axis=0) * p.scale)[0:1, : p.experts]

    for j in range(1, NZ):
        meta_copy(j).wait_send()
        first_copy(j).wait_send()
        d_copy(j).wait_send()

    def settle(f):
        for k in range(K):
            pl.when(f > 0)(tok_copy(f, k).wait_send)
            pl.when(f < N - 1)(c_copy(f, k).wait_send)
        for j in range(1, NY):
            y_copy(f, j).wait_send()
            b_copy(f, j).wait_send()
        for n in range(6):
            x_copy(f, n).wait_send()

    every(0, N, settle)
    for copy in w_copies:
        copy.wait_send()
    for n in range(6):
        h_copy(n).wait_send()
    for j in range(1, NY):
        load_copy(j).wait_send()


def shards(nz, ny, tokens, route_slots, route_scores, slot_expert, w_in, w_out):
    tok, width = tokens.shape
    top = route_slots.shape[1]
    _, full, _, hidden = w_in.shape
    slots = nz * ny
    experts = slots - slots // 4
    p = Plan(nz, ny, tok, top, width, hidden, experts, experts / (slots * tok * ROUTED))
    bf, f32 = jnp.bfloat16, jnp.float32
    dma = pltpu.SemaphoreType.DMA
    R, A, N, C, L = p.rows, p.all_rows, p.cuts, p.cut, nz * tok
    vmem = pl.BlockSpec(memory_space=pltpu.VMEM)
    smem = pl.BlockSpec(memory_space=pltpu.SMEM)
    anyspace = pl.BlockSpec(memory_space=pl.ANY)
    return pl.pallas_call(
        functools.partial(layer_kernel, p),
        out_shape=(
            jax.ShapeDtypeStruct((tok, width), bf),
            jax.ShapeDtypeStruct((1, experts), f32),
        ),
        in_specs=[vmem, vmem, vmem, smem, anyspace, anyspace],
        out_specs=(vmem, vmem),
        scratch_shapes=[
            pltpu.VMEM((N, nz, tok, C), bf),
            pltpu.VMEM((nz, 2 * top, 2 * tok), f32),
            pltpu.VMEM((L, L), bf),
            pltpu.VMEM((A, L), bf),
            pltpu.VMEM((A, L), f32),
            pltpu.VMEM((L, A), bf),
            pltpu.VMEM((N, ny, R, C), bf),
            pltpu.VMEM((4, N, ny, R, C), bf),
            pltpu.VMEM((A, 2 * hidden), f32),
            pltpu.VMEM((4, A, hidden), bf),
            pltpu.VMEM((4, hidden, width), bf),
            pltpu.VMEM((2, hidden // 2, width), bf),
            pltpu.VMEM((full, 2, hidden), bf),
            pltpu.VMEM((full, 2 * hidden), bf),
            pltpu.VMEM((N, ny, R, C), bf),
            pltpu.VMEM((N, ny, R, C), bf),
            pltpu.VMEM((N, nz, tok, C), f32),
            pltpu.VMEM((N, nz, tok, C), bf),
            pltpu.VMEM((N, nz, tok, C), bf),
            pltpu.VMEM((nz, tok, C), bf),
            pltpu.VMEM((nz, tok, C), bf),
            pltpu.VMEM((ny, 8, 128), f32),
            dma((N, p.levels)), dma((N, p.levels)),
            dma((nz,)), dma((nz,)),
            dma((N, ny)), dma((N, ny)),
            dma((N, 6)), dma((N, 6)),
            dma((6,)), dma((6,)),
            dma((6,)), dma((6,)),
            dma((N, ny)), dma((N, ny)),
            dma((N, p.levels)), dma((N, p.levels)),
            dma((nz,)), dma((nz,)),
            dma((nz,)), dma((nz,)),
            dma((ny,)), dma((ny,)),
            dma((2,)),
        ],
        compiler_params=pltpu.CompilerParams(
            collective_id=0, has_side_effects=True, vmem_limit_bytes=60 * 1024 * 1024
        ),
    )(tokens, route_slots.T, route_scores.T, slot_expert, w_in[0], w_out[0])


def solution(mesh, nz=8):
    ny = mesh.shape["expert"] // nz
    placed = (
        P(("dp", "expert"), "tensor"),
        P(("dp", "expert"), None),
        P(("dp", "expert"), None),
        P(),
        P("expert", None, None, "tensor"),
        P("expert", "tensor", None),
    )
    return jax.shard_map(
        functools.partial(shards, nz, ny),
        mesh=mesh,
        in_specs=placed,
        out_specs=(P(("dp", "expert"), "tensor"), P("dp", None)),
        check_vma=False,
    )
```

```python
import functools

import jax
import jax.numpy as jnp
from jax import lax
from jax.experimental import pallas as pl
from jax.experimental.pallas import tpu as pltpu
from jax.sharding import PartitionSpec as P

ROUTED = 2.5
MESH = pl.DeviceIdType.MESH


class Plan:
    def __init__(self, nz, ny, tok, top, width, hidden, experts, scale):
        self.nz, self.ny, self.tok, self.top = nz, ny, tok, top
        self.slots = nz * ny
        self.cap = 9 * tok * top // (8 * self.slots)
        self.rows = nz * self.cap
        self.all_rows = ny * self.rows
        self.width, self.hidden = width, hidden
        self.experts, self.scale = experts, scale
        self.cut = 128
        self.cuts = width // self.cut
        self.levels = nz.bit_length() - 1


def layer_kernel(
    p,
    tok_ref, slots_ref, scores_ref, held_ref, win_ref, wout_ref,
    out_ref, load_ref,
    tokens, metas, before, sel, selg, selgt, outgo, gath, proj, hid, wcols, relay, wraw, wfirst,
    result, back, part, carry, passed, carry_last, passed_last, loads,
    z_send, z_recv, m_send, m_recv, y_send, y_recv, x_send, x_recv,
    h_send, h_recv, w_send, w_recv, b_send, b_recv, c_send, c_recv, d_send, d_recv, l_send, l_recv, own,
):
    NZ, NY, T = p.nz, p.ny, p.tok
    W, F, C, N = p.width, p.hidden, p.cut, p.cuts
    L = NZ * T
    e = lax.axis_index("expert")
    x = lax.axis_index("tensor")
    z = e // NY
    y = e % NY
    right, left, across = (x + 1) % 4, (x + 3) % 4, (x + 2) % 4
    HY = NY // 2
    K = p.levels
    far = [NZ >> (k + 1) for k in range(K)]
    bits = [z // far[k] % 2 for k in range(K)]
    spot = sum(bits[k] * (1 << k) for k in range(K))
    mate = [z + far[k] * (1 - 2 * bits[k]) for k in range(K)]

    def line_place(r):
        return sum(r // (1 << k) % 2 * far[k] for k in range(K))


    def remote(src, dst, send, recv, dev):
        return pltpu.make_async_remote_copy(
            src_ref=src, dst_ref=dst, send_sem=send, recv_sem=recv, device_id=dev, device_id_type=MESH
        )

    def arrive(dst, recv):
        remote(dst, dst, recv, recv, {"tensor": right}).wait_recv()

    def at_z(k):
        return {"expert": k * NY + y}

    def at_y(k):
        return {"expert": z * NY + k}

    def every(lo, hi, body):
        def step(i, c):
            body(i)
            return c

        lax.fori_loop(lo, hi, step, 0)

    barrier = pltpu.get_barrier_semaphore()

    for j in range(1, NZ):
        pl.semaphore_signal(barrier, inc=1, device_id=at_z((z + j) % NZ), device_id_type=MESH)
    for j in range(1, NY):
        pl.semaphore_signal(barrier, inc=1, device_id=at_y((y + j) % NY), device_id_type=MESH)
    for n in (right, left):
        pl.semaphore_signal(barrier, inc=1, device_id={"tensor": n}, device_id_type=MESH)

    own_wcols = pltpu.make_async_copy(wout_ref.at[:, pl.ds(pl.multiple_of(x * W, 128), W)], wcols.at[x], own.at[0])
    own_win = pltpu.make_async_copy(win_ref, wraw, own.at[1])
    own_wcols.start()
    own_win.start()

    scores = scores_ref[...]
    gates = scores / jnp.sum(scores, axis=0, keepdims=True) * ROUTED
    names = slots_ref[...].astype(jnp.float32)
    for at in (0, T):
        metas[spot, : p.top, at : at + T] = names
        metas[spot, p.top :, at : at + T] = gates
    for f in range(N):
        tokens[f, spot] = tok_ref[:, f * C : (f + 1) * C]

    i0 = lax.broadcasted_iota(jnp.int32, (L, L), 0)
    i1 = lax.broadcasted_iota(jnp.int32, (L, L), 1)
    before[...] = jnp.where((i0 < i1) & (i0 // T == i1 // T), 1.0, 0.0).astype(jnp.bfloat16)
    proj[...] = jnp.zeros_like(proj)
    pl.semaphore_wait(barrier, NY - 1 + 2 + NZ - 1)

    def held_at(k):
        return pl.ds(spot // (1 << k) * (1 << k), 1 << k)

    def coming_at(k):
        return pl.ds(spot // (2 << k) * (2 << k) + (1 - bits[k]) * (1 << k), 1 << k)

    def meta_copy(j):
        ref = metas.at[spot]
        return remote(ref, ref, m_send.at[j], m_recv.at[j], at_z(line_place((spot + j) % NZ)))

    def tok_copy(f, k):
        ref = tokens.at[f, held_at(k)]
        return remote(ref, ref, z_send.at[f, k], z_recv.at[f, k], at_z(mate[k]))

    def wblock(k, r0, n):
        return wout_ref.at[pl.ds(r0, n), pl.ds(pl.multiple_of(k * W, 128), W)]

    FH = F // 2
    w_copies = [
        remote(wblock(across, 0, FH), relay.at[0], w_send.at[0], w_recv.at[0], {"tensor": right}),
        remote(wblock(across, FH, FH), relay.at[1], w_send.at[1], w_recv.at[1], {"tensor": left}),
        remote(wblock(right, 0, F), wcols.at[x], w_send.at[2], w_recv.at[2], {"tensor": right}),
        remote(wblock(left, 0, F), wcols.at[x], w_send.at[3], w_recv.at[3], {"tensor": left}),
        remote(relay.at[0], wcols.at[left, pl.ds(0, FH)], w_send.at[4], w_recv.at[4], {"tensor": right}),
        remote(relay.at[1], wcols.at[right, pl.ds(FH, FH)], w_send.at[5], w_recv.at[5], {"tensor": left}),
    ]

    def line_routes():
        lane = lax.broadcasted_iota(jnp.int32, (p.top, 2 * T), 1)
        slots, gates = [], []
        for k in range(0, NZ, 2):
            a, b = metas[k], metas[k + 1]
            slots.append(jnp.where(lane < T, a[: p.top], b[: p.top]))
            gates.append(jnp.where(lane < T, a[p.top :], b[p.top :]))
        return jnp.concatenate(slots, axis=1).astype(jnp.int32), jnp.concatenate(gates, axis=1)

    def choose():
        slots, gates = line_routes()
        mine = lax.broadcasted_iota(jnp.int32, (NY, L), 0) + z * NY
        match = jnp.zeros((NY, L), jnp.float32)
        gate = jnp.zeros((NY, L), jnp.float32)
        for k in range(p.top):
            eq = slots[k : k + 1] == mine
            match = match + jnp.where(eq, 1.0, 0.0)
            gate = gate + jnp.where(eq, gates[k : k + 1], 0.0)
        rank = jnp.dot(match.astype(jnp.bfloat16), before[...], preferred_element_type=jnp.float32)
        block = lax.broadcasted_iota(jnp.int32, (NY, L), 1) // T
        key = jnp.where(match > 0.5, rank.astype(jnp.int32) * NZ + block, -1)
        place = lax.broadcasted_iota(jnp.int32, (p.rows, L), 0)
        for k in range(NY):
            hit = key[k : k + 1] == place
            rows = pl.ds(k * p.rows, p.rows)
            sel[rows] = jnp.where(hit, 1.0, 0.0).astype(jnp.bfloat16)
            selg[rows] = jnp.where(hit, gate[k : k + 1], 0.0)

    def load_copy(j):
        return remote(loads.at[y], loads.at[y], l_send.at[j], l_recv.at[j], at_y((y + j) % NY))

    def weigh():
        slots, gates = line_routes()
        names = lax.broadcasted_iota(jnp.int32, (p.slots, L), 0)
        total = jnp.zeros((p.slots, L), jnp.float32)
        for k in range(p.top):
            total = total + jnp.where(slots[k : k + 1] == names, gates[k : k + 1], 0.0)
        total = jnp.broadcast_to(jnp.sum(total, axis=1, keepdims=True), (p.slots, 128))
        expert = lax.broadcasted_iota(jnp.int32, (1, 128), 1)
        row = jnp.zeros((1, 128), jnp.float32)
        for s in range(p.slots):
            row = row + jnp.where(expert == held_ref[s], total[s : s + 1], 0.0)
        loads[y] = jnp.broadcast_to(row, (8, 128))
        for j in range(1, NY):
            load_copy(j).start()
        selgt[...] = jnp.transpose(selg[...], (1, 0)).astype(jnp.bfloat16)

    def y_copy(f, j):
        k = (y + j) % NY
        return remote(outgo.at[f, k], gath.at[x, f, y], y_send.at[f, j], y_recv.at[f, j], at_y(k))

    def y_out(f):
        rows = jnp.dot(sel[...], tokens[f].reshape(L, C), preferred_element_type=jnp.float32)
        outgo[f] = rows.astype(jnp.bfloat16).reshape(NY, p.rows, C)
        for j in range(1, NY):
            y_copy(f, j).start()
        gath[x, f, y] = outgo[f, y]

    def half(o, f, low):
        return gath.at[o, f, pl.ds(0 if low else HY, HY)]

    def x_copy(f, n):
        o, low, to = (
            (x, True, right), (x, False, left), (x, False, right), (x, True, left), (left, True, right), (right, False, left)
        )[n]
        return remote(half(o, f, low), half(o, f, low), x_send.at[f, n], x_recv.at[f, n], {"tensor": to})

    def x_arrive(f, n):
        o, low = ((left, True), (right, False), (left, False), (right, True), (across, True), (across, False))[n]
        arrive(half(o, f, low), x_recv.at[f, n])

    def x_out(f):
        for j in range(1, NY):
            arrive(gath.at[x, f, (y - j + NY) % NY], y_recv.at[f, j])
        for n in range(4):
            x_copy(f, n).start()

    def x_pass(f):
        x_arrive(f, 0)
        x_copy(f, 4).start()
        x_arrive(f, 1)
        x_copy(f, 5).start()

    def project(f):
        for n in range(2, 6):
            x_arrive(f, n)

        def add_up(first, n):
            total = proj[...]
            for o in range(4):
                rows = [gath[o, first + i].reshape(p.all_rows, C) for i in range(n)]
                total = total + jnp.dot(
                    rows[0] if n == 1 else jnp.concatenate(rows, axis=1),
                    wfirst[pl.ds(pl.multiple_of(o * W + first * C, C), n * C), :],
                    preferred_element_type=jnp.float32,
                )
            proj[...] = total

        pl.when(f % 2 == 1)(lambda: add_up(f - 1, 2))
        if N % 2:
            pl.when(f == N - 1)(lambda: add_up(f, 1))

    def tell_apart(i):
        def part_of(j):
            r0 = pl.multiple_of((i * 4 + j) * C, C)
            pairs = wraw[pl.ds(r0, C)].reshape(2 * C, F)
            row = lax.broadcasted_iota(jnp.int32, (C, 2 * C), 0)
            col = lax.broadcasted_iota(jnp.int32, (C, 2 * C), 1)
            for g in (0, 1):
                pick = jnp.where(col == 2 * row + g, 1.0, 0.0).astype(jnp.bfloat16)
                got = jnp.dot(pick, pairs, preferred_element_type=jnp.float32)
                wfirst[pl.ds(r0, C), g * F : (g + 1) * F] = got.astype(jnp.bfloat16)

        every(0, 4, part_of)

    for j in range(1, NZ):
        meta_copy(j).start()
    own_win.wait()

    LZ = [2 * k for k in range(K)]
    LY = LZ[-1] + 2
    LX = LY + 2
    LP = LX + 1
    LM = LP + 1

    def tick(t):
        for k in range(K):
            @pl.when((t >= LZ[k]) & (t < LZ[k] + N))
            def _(k=k):
                f = t - LZ[k]
                if k:
                    arrive(tokens.at[f, coming_at(k - 1)], z_recv.at[f, k - 1])
                tok_copy(f, k).start()

        @pl.when(t == 1)
        def _():
            for copy in w_copies[:4]:
                copy.start()

        @pl.when(t < 5)
        def _():
            every(jnp.where(t < 2, 2 * t, t + 2), jnp.minimum(jnp.where(t < 2, 2 * t + 2, t + 3), N), tell_apart)

        @pl.when(t == LY - 1)
        def _():
            for j in range(1, NZ):
                arrive(metas.at[(spot - j + NZ) % NZ], m_recv.at[j])
            choose()

        @pl.when((t >= LY) & (t < LY + N))
        def _():
            arrive(tokens.at[t - LY, coming_at(K - 1)], z_recv.at[t - LY, K - 1])
            y_out(t - LY)

        @pl.when(t == LX)
        def _():
            for n in (0, 1):
                arrive(relay.at[n], w_recv.at[n])
                w_copies[4 + n].start()

        @pl.when((t >= LX) & (t < LX + N))
        def _():
            x_out(t - LX)

        @pl.when((t >= LP) & (t < LP + N))
        def _():
            x_pass(t - LP)

        @pl.when((t >= LM) & (t < LM + N))
        def _():
            project(t - LM)

    every(0, LM + N, tick)

    gate_part = proj[:, :F]
    value = gate_part / (1.0 + jnp.exp(-gate_part)) * proj[:, F:]
    hid[x] = value.astype(jnp.bfloat16)
    HR = p.all_rows // 2

    def h_half(o, low):
        return hid.at[o, pl.ds(0 if low else HR, HR)]

    def h_copy(n):
        o, low, to = (
            (x, True, right), (x, False, left), (x, False, right), (x, True, left), (left, True, right), (right, False, left)
        )[n]
        return remote(h_half(o, low), h_half(o, low), h_send.at[n], h_recv.at[n], {"tensor": to})

    def h_arrive(n):
        o, low = ((left, True), (right, False), (left, False), (right, True), (across, True), (across, False))[n]
        arrive(h_half(o, low), h_recv.at[n])

    for n in range(4):
        h_copy(n).start()
    h_arrive(0)
    h_copy(4).start()
    h_arrive(1)
    h_copy(5).start()
    weigh()
    arrive(wcols.at[left], w_recv.at[2])
    arrive(wcols.at[right], w_recv.at[3])
    arrive(wcols.at[across, pl.ds(0, FH)], w_recv.at[4])
    arrive(wcols.at[across, pl.ds(FH, FH)], w_recv.at[5])
    own_wcols.wait()
    for n in range(2, 6):
        h_arrive(n)

    def b_copy(f, j):
        k = (y + j) % NY
        return remote(result.at[f, k], back.at[f, y], b_send.at[f, j], b_recv.at[f, j], at_y(k))

    def expand(first, n):
        total = jnp.zeros((p.all_rows, n * C), jnp.float32)
        for o in range(4):
            total = total + jnp.dot(
                hid[o], wcols[o, :, first * C : (first + n) * C], preferred_element_type=jnp.float32
            )
        total = total.astype(jnp.bfloat16)
        for i in range(n):
            f = first + i
            result[f] = total[:, i * C : (i + 1) * C].reshape(NY, p.rows, C)
            for j in range(1, NY):
                b_copy(f, j).start()
            back[f, y] = result[f, y]

    if N % 2:
        expand(0, 1)
    for f in range(N % 2, N, 2):
        expand(f, 2)

    def combine(f):
        for j in range(1, NY):
            arrive(back.at[f, (y - j + NY) % NY], b_recv.at[f, j])
        value = jnp.dot(selgt[...], back[f].reshape(p.all_rows, C), preferred_element_type=jnp.float32)
        part[f] = value.reshape(NZ, T, C)
        pl.when(f < N - 1)(lambda: pass_on(f, K - 1))

        @pl.when(f == N - 1)
        def _():
            passed_last[...] = part[f].astype(jnp.bfloat16)
            for j in range(1, NZ):
                d_copy(j).start()

    def d_copy(j):
        to = (spot + j) % NZ
        return remote(passed_last.at[to], carry_last.at[spot], d_send.at[j], d_recv.at[j], at_z(line_place(to)))

    def last_in():
        total = part[N - 1, spot]
        for j in range(1, NZ):
            k = (spot - j + NZ) % NZ
            arrive(carry_last.at[k], d_recv.at[j])
            total = total + carry_last[k].astype(jnp.float32)
        out_ref[:, (N - 1) * C :] = total.astype(jnp.bfloat16)

    def c_copy(f, k):
        ref = pl.ds(1 << k, 1 << k)
        return remote(passed.at[f, ref], carry.at[f, ref], c_send.at[f, k], c_recv.at[f, k], at_z(mate[k]))

    def pass_on(f, k):
        passed[f, (1 << k) : (2 << k)] = part[f, coming_at(k)].astype(jnp.bfloat16)
        c_copy(f, k).start()

    def take_in(f, k):
        arrive(carry.at[f, pl.ds(1 << k, 1 << k)], c_recv.at[f, k])
        total = part[f, held_at(k)] + carry[f, (1 << k) : (2 << k)].astype(jnp.float32)
        if k:
            part[f, held_at(k)] = total
            pass_on(f, k - 1)
        else:
            out_ref[:, pl.ds(pl.multiple_of(f * C, C), C)] = total[0].astype(jnp.bfloat16)

    def back_tick(t):
        @pl.when(t < N)
        def _():
            combine(t)

        for i in range(K):
            @pl.when((t >= 2 * i + 2) & (t < 2 * i + 1 + N))
            def _(i=i):
                take_in(t - 2 * i - 2, K - 1 - i)

    every(0, 2 * K + N - 1, back_tick)
    last_in()

    for j in range(1, NY):
        arrive(loads.at[(y - j + NY) % NY], l_recv.at[j])
    load_ref[...] = (jnp.sum(loads[...], axis=0) * p.scale)[0:1, : p.experts]

    for j in range(1, NZ):
        meta_copy(j).wait_send()
        d_copy(j).wait_send()

    def settle(f):
        for k in range(K):
            tok_copy(f, k).wait_send()
            pl.when(f < N - 1)(c_copy(f, k).wait_send)
        for j in range(1, NY):
            y_copy(f, j).wait_send()
            b_copy(f, j).wait_send()
        for n in range(6):
            x_copy(f, n).wait_send()

    every(0, N, settle)
    for copy in w_copies:
        copy.wait_send()
    for n in range(6):
        h_copy(n).wait_send()
    for j in range(1, NY):
        load_copy(j).wait_send()


def shards(nz, ny, tokens, route_slots, route_scores, slot_expert, w_in, w_out):
    tok, width = tokens.shape
    top = route_slots.shape[1]
    _, full, _, hidden = w_in.shape
    slots = nz * ny
    experts = slots - slots // 4
    p = Plan(nz, ny, tok, top, width, hidden, experts, experts / (slots * tok * ROUTED))
    bf, f32 = jnp.bfloat16, jnp.float32
    dma = pltpu.SemaphoreType.DMA
    R, A, N, C, L = p.rows, p.all_rows, p.cuts, p.cut, nz * tok
    vmem = pl.BlockSpec(memory_space=pltpu.VMEM)
    smem = pl.BlockSpec(memory_space=pltpu.SMEM)
    anyspace = pl.BlockSpec(memory_space=pl.ANY)
    return pl.pallas_call(
        functools.partial(layer_kernel, p),
        out_shape=(
            jax.ShapeDtypeStruct((tok, width), bf),
            jax.ShapeDtypeStruct((1, experts), f32),
        ),
        in_specs=[vmem, vmem, vmem, smem, anyspace, anyspace],
        out_specs=(vmem, vmem),
        scratch_shapes=[
            pltpu.VMEM((N, nz, tok, C), bf),
            pltpu.VMEM((nz, 2 * top, 2 * tok), f32),
            pltpu.VMEM((L, L), bf),
            pltpu.VMEM((A, L), bf),
            pltpu.VMEM((A, L), f32),
            pltpu.VMEM((L, A), bf),
            pltpu.VMEM((N, ny, R, C), bf),
            pltpu.VMEM((4, N, ny, R, C), bf),
            pltpu.VMEM((A, 2 * hidden), f32),
            pltpu.VMEM((4, A, hidden), bf),
            pltpu.VMEM((4, hidden, width), bf),
            pltpu.VMEM((2, hidden // 2, width), bf),
            pltpu.VMEM((full, 2, hidden), bf),
            pltpu.VMEM((full, 2 * hidden), bf),
            pltpu.VMEM((N, ny, R, C), bf),
            pltpu.VMEM((N, ny, R, C), bf),
            pltpu.VMEM((N, nz, tok, C), f32),
            pltpu.VMEM((N, nz, tok, C), bf),
            pltpu.VMEM((N, nz, tok, C), bf),
            pltpu.VMEM((nz, tok, C), bf),
            pltpu.VMEM((nz, tok, C), bf),
            pltpu.VMEM((ny, 8, 128), f32),
            dma((N, p.levels)), dma((N, p.levels)),
            dma((nz,)), dma((nz,)),
            dma((N, ny)), dma((N, ny)),
            dma((N, 6)), dma((N, 6)),
            dma((6,)), dma((6,)),
            dma((6,)), dma((6,)),
            dma((N, ny)), dma((N, ny)),
            dma((N, p.levels)), dma((N, p.levels)),
            dma((nz,)), dma((nz,)),
            dma((ny,)), dma((ny,)),
            dma((2,)),
        ],
        compiler_params=pltpu.CompilerParams(
            collective_id=0, has_side_effects=True, vmem_limit_bytes=60 * 1024 * 1024
        ),
    )(tokens, route_slots.T, route_scores.T, slot_expert, w_in[0], w_out[0])


def solution(mesh, nz=8):
    ny = mesh.shape["expert"] // nz
    placed = (
        P(("dp", "expert"), "tensor"),
        P(("dp", "expert"), None),
        P(("dp", "expert"), None),
        P(),
        P("expert", None, None, "tensor"),
        P("expert", "tensor", None),
    )
    return jax.shard_map(
        functools.partial(shards, nz, ny),
        mesh=mesh,
        in_specs=placed,
        out_specs=(P(("dp", "expert"), "tensor"), P("dp", None)),
        check_vma=False,
    )
```
